32 devices in a mesh: row: 8 (over y, x, core), col: 4 (over z).
Axes of the slice: x: 2, y: 2, z: 4, core: 2. Of those that a mesh axis runs over, the one named last changes fastest.
Arguments:
- student_in: bfloat16 [768, 8192], P('col', 'row'), may hold values from -6 to 6
- norm_gain: bfloat16 [8192], P('row'), may hold values from 0.099609375 to 1.8984375
- w_gate: bfloat16 [8192, 28672], P('row', 'col'), may hold values from -0.0625 to 0.0625
- w_up: bfloat16 [8192, 28672], P('row', 'col'), may hold values from -0.0625 to 0.0625
- w_down: bfloat16 [28672, 8192], P('col', 'row'), may hold values from -0.03125 to 0.03125
- teacher: bfloat16 [2, 768, 8192], P(None, 'col', 'row'), may hold values from -6 to 6
- layer_map: int32 [2], replicated, may hold values from 0 to 1, each once
Outputs:
- student_out: bfloat16 [768, 8192], P('col', 'row')
- match_loss: float32 [], replicated
The draws below stay inside these ranges and needn't reach their ends.
Inputs may be any that keep to these rules, and one draw needn't show every extreme that they name: `layer_map`: a permutation of 0 to 1.
All inputs are finite; a program needn't handle non-finite values.
Results may differ from the reference program's by a relative error of at most 0.014.
Values may be sent and summed in bfloat16 or wider, within the bound.
A program may use at most 192 MiB of HBM per device.

```python
import jax
import jax.numpy as jnp
from jax import lax

D = 8192
FF = 28672
TEACH = 2
TOKENS = 768
N_ROW = 8
N_COL = 4


def level_of(key, shape, split, smallest, top_value):
    factor_of = 1.0
    for position, parts in split:
        heights = jax.random.uniform(jax.random.fold_in(jax.random.fold_in(key, 6), position), (parts,), jnp.float32, smallest / len(split), top_value / len(split))
        factor_of = factor_of * jnp.repeat(jnp.exp(heights), shape[position] // parts).reshape((-1,) + (1,) * (len(shape) - 1 - position))
    return factor_of


def gaussian(rng, extent, deviation, most, pieces=(), dtype=jnp.bfloat16):
    loudness = level_of(rng, extent, pieces, -0.22, 0.18) if pieces else 1.0
    array = jax.random.normal(rng, extent, jnp.float32) * deviation * loudness
    return jnp.minimum(jnp.maximum(array, -most), most).astype(dtype)


def setup_inputs(seed: int = 0) -> dict:
    streams_of = jax.random.split(jax.random.key(seed), 8)
    return {
        "student_in": gaussian(streams_of[0], (TOKENS, D), 1.0, 6.0, ((0, 4), (1, 8))),
        "norm_gain": jnp.clip(1.0 + 0.18 * jax.random.normal(streams_of[1], (D,), jnp.float32), 0.099609375, 1.8984375).astype(jnp.bfloat16),
        "w_gate": gaussian(streams_of[2], (D, FF), D ** -0.5, 0.0625, ((0, 8), (1, 4))),
        "w_up": gaussian(streams_of[3], (D, FF), D ** -0.5, 0.0625, ((0, 8), (1, 4))),
        "w_down": gaussian(streams_of[4], (FF, D), FF ** -0.5, 0.03125, ((0, 4), (1, 8))),
        "teacher": gaussian(streams_of[5], (TEACH, TOKENS, D), 1.0, 6.0, ((1, 4), (2, 8))),
        "layer_map": jax.random.permutation(streams_of[6], TEACH).astype(jnp.int32),
    }


def reference(student_in, norm_gain, w_gate, w_up, w_down, teacher, layer_map):
    xf = student_in.astype(jnp.float32)
    mean_sq = lax.optimization_barrier(jnp.mean(xf * xf, axis=1, keepdims=True))
    normed = (xf * jax.lax.rsqrt(mean_sq + 1e-05) * norm_gain.astype(jnp.float32)[None, :]).astype(jnp.bfloat16)
    feat_block = D // N_ROW
    gate = jnp.zeros((normed.shape[0], FF), jnp.float32)
    up = jnp.zeros((normed.shape[0], FF), jnp.float32)
    for index in range(N_ROW):
        cols = normed[:, index * feat_block:(index + 1) * feat_block]
        gate = gate + jnp.dot(cols, w_gate[index * feat_block:(index + 1) * feat_block], preferred_element_type=jnp.float32).astype(jnp.bfloat16).astype(jnp.float32)
        up = up + jnp.dot(cols, w_up[index * feat_block:(index + 1) * feat_block], preferred_element_type=jnp.float32).astype(jnp.bfloat16).astype(jnp.float32)
    hidden = (jax.nn.silu(gate) * up).astype(jnp.bfloat16)
    hid_block = FF // N_COL
    branch = jnp.zeros((normed.shape[0], D), jnp.float32)
    for index in range(N_COL):
        part = jnp.dot(hidden[:, index * hid_block:(index + 1) * hid_block], w_down[index * hid_block:(index + 1) * hid_block], preferred_element_type=jnp.float32)
        branch = branch + part.astype(jnp.bfloat16).astype(jnp.float32)
    student_out = (xf + branch).astype(jnp.bfloat16)
    target = jax.lax.dynamic_index_in_dim(teacher, layer_map[0].astype(jnp.int32), 0, keepdims=False).astype(jnp.float32)
    diff = student_out.astype(jnp.float32) - target
    match_loss = jnp.mean(diff * diff)
    return (student_out, match_loss)
```

```python
import functools

import jax
import jax.numpy as jnp
from jax import lax
from jax.experimental import pallas as pl
from jax.experimental.pallas import tpu as pltpu
from jax.sharding import PartitionSpec as P

BF = jnp.bfloat16
F32 = jnp.float32
LAG = 2
SLOTS = 4


def kernel(nr, nz, w, total, lead, x_ref, gain_ref, wg_ref, wu_ref, wd_ref, teacher_ref, map_ref,
           out_ref, loss_ref,
           xg, ss, ssr, scr, scale, wgu, wdn, p_own, p_send, s_in, half_send, half_in,
           full_send, full_in, h_all, acc, cs, cr, lsum, l_row, l_col,
           x_sems, w_sem, wd_sem, ss_sems, sc_sems, sib_sems, rs_send, rs_recv, ag_send, ag_recv,
           hs_sems, c_sems, l_sems):
    items = s_in.shape[0]
    n = nr // 2
    hn = n // 2
    m, feat = x_ref.shape
    mp = ss.shape[-1]
    g = m // n
    hw = w // 2
    chunks = items // nz
    r = lax.axis_index("row")
    z = lax.axis_index("col")
    core = lax.rem(r, 2)
    chip = lax.div(r, 2)
    a, b = lax.div(chip, 2), lax.rem(chip, 2)
    pos = a + b * (n - 1 - 2 * a)

    def chip_at(off):
        q = lax.rem(pos + (off % n), n)
        far = lax.div(q, hn)
        return far * (2 * (n - 1 - q) + 1) + (1 - far) * 2 * q

    me = chip_at(0)
    sibling = {"row": chip * 2 + 1 - core}
    ring = ({"row": chip_at(1) * 2 + core}, {"row": chip_at(-1) * 2 + core})
    sign = (1, -1)
    pair_of = (slice(0, hw), slice(hw, w))
    unit_of = (pl.ds(0, hw // 2), pl.ds(hw // 2, hw // 2))
    masks = [0] + list(range(2, nz)) + [1]

    def plane(k, back=False):
        if nz & (nz - 1):
            return lax.rem(z + (nz - k if back else k), nz)
        q, bit = z, 1
        while bit <= masks[k]:
            if masks[k] & bit:
                q = q + bit * (1 - 2 * lax.rem(lax.div(z, bit), 2))
            bit *= 2
        return q

    def remote(src, dst, send, recv, dev):
        return pltpu.make_async_remote_copy(
            src_ref=src, dst_ref=dst, send_sem=send, recv_sem=recv,
            device_id=dev, device_id_type=pl.DeviceIdType.MESH)

    barrier = pltpu.get_barrier_semaphore()
    for d in range(1, nr):
        pl.semaphore_signal(barrier, inc=1, device_id={"row": lax.rem(r + d, nr)},
                            device_id_type=pl.DeviceIdType.MESH)
    for d in range(1, nz):
        pl.semaphore_signal(barrier, inc=1, device_id={"col": lax.rem(z + d, nz)},
                            device_id_type=pl.DeviceIdType.MESH)

    def where(j):
        v = j + (chunks - lead)
        return lax.rem(lax.div(v, chunks), nz), lax.rem(v, chunks)

    def up_load(j):
        slot = lax.rem(j, 2)
        copies = []
        for part, c in enumerate((1 - core, core)):
            cols = pl.ds(pl.multiple_of(where(j)[1] * w + c * hw, hw), hw)
            for u, ref in enumerate((wg_ref, wu_ref)):
                copies.append(pltpu.make_async_copy(
                    ref.at[:, cols], wgu.at[slot, 2 * part + u], w_sem.at[slot, 2 * part + u]))
        return copies

    def down_load(j):
        slot = lax.rem(j, 2)
        return pltpu.make_async_copy(
            wd_ref.at[pl.ds(pl.multiple_of(where(j)[1] * w, w), w)], wdn.at[slot], wd_sem.at[slot])

    for c in up_load(jnp.int32(0)):
        c.start()
    down_load(jnp.int32(0)).start()

    xf = x_ref[...].astype(F32)
    xg[0] = (xf * gain_ref[...].astype(F32)).astype(BF)
    sq = xf * xf
    part = sq[:, 0:128]
    for c in range(1, feat // 128):
        part = part + sq[:, c * 128:(c + 1) * 128]
    part = jnp.sum(part, axis=1, keepdims=True)
    same = lax.broadcasted_iota(jnp.int32, (m, mp), 0) == lax.broadcasted_iota(jnp.int32, (m, mp), 1)
    ss[...] = jnp.sum(jnp.where(same, part, 0.0), axis=0, keepdims=True)

    pl.semaphore_wait(barrier, nr - 1 + nz - 1)

    def x_copy(k, back=False):
        return remote(xg.at[0], xg.at[k], x_sems.at[0, k - 1], x_sems.at[1, k - 1],
                      {"col": plane(k, not back)})

    def x_wait(k):
        ref = xg.at[k]
        remote(ref, ref, x_sems.at[0, k - 1], x_sems.at[1, k - 1], {"col": plane(1)}).wait_recv()

    def ss_copy(d):
        return remote(ss, ssr.at[d - 1], ss_sems.at[0, d - 1], ss_sems.at[1, d - 1],
                      {"row": lax.rem(r + d, nr)})

    def scale_copy(k):
        return remote(scr.at[0], scr.at[k], sc_sems.at[0, k - 1], sc_sems.at[1, k - 1],
                      {"col": plane(k, True)})

    for d in range(1, nr):
        ss_copy(d).start()
    if nz > 1:
        x_copy(1).start()
    acc[0] = x_ref[...].astype(F32)
    for k in range(1, nz):
        acc[k] = jnp.zeros_like(acc[k])

    def sib(j):
        slot = lax.rem(j, 2)
        return remote(p_send.at[slot], s_in.at[j], sib_sems.at[slot], sib_sems.at[2 + j], sibling)

    def rs(s, d, j):
        slot = lax.rem(j, SLOTS)
        if s == 0:
            src, dst = half_send.at[slot, d], half_in.at[j, d]
        else:
            src, dst = full_send.at[slot, s - 1, d], full_in.at[j, s - 1, d]
        return remote(src, dst, rs_send.at[s, d, slot], rs_recv.at[s, d, j], ring[d])

    def ag(s, d, j, got=False):
        blk = chip_at(-sign[d] * (s + 1 if got else s))
        ref = h_all.at[j, core, blk]
        if s == hn - 1:
            ref = h_all.at[j, core, blk, :, unit_of[d]]
        return remote(ref, ref, ag_send.at[s, d, lax.rem(j, SLOTS)], ag_recv.at[s, d, j], ring[d])

    def hs(j, got=False):
        ref = h_all.at[j, 1 - core if got else core]
        return remote(ref, ref, hs_sems.at[lax.rem(j, SLOTS)], hs_sems.at[SLOTS + j], sibling)

    def free(make, j, slots=SLOTS):
        @pl.when(j >= slots)
        def _():
            make(j - slots).wait_send()

    def mine(j, off, cols=slice(None)):
        q = chip_at(off)
        slot = lax.rem(j, p_own.shape[0])
        return p_own[slot, q, :, cols].astype(F32) + s_in[j, q, :, cols].astype(F32)

    def first(j):
        slot = lax.rem(j, 2)
        k, chunk = where(j)

        @pl.when(j + 1 < items)
        def _():
            for c in up_load(j + 1):
                c.start()

        @pl.when((chunk == 0) & (k > 0))
        def _():
            x_wait(k)
        for c in up_load(j):
            c.wait()
        free(sib, j, 2)
        for i in range(4):
            res = jnp.dot(xg[k], wgu[slot, i], preferred_element_type=F32).astype(BF).reshape(n, g, hw)
            if i < 2:
                p_send[slot, :, :, pair_of[i]] = res
            else:
                p_own[lax.rem(j, p_own.shape[0]), :, :, pair_of[i - 2]] = res
            if i == 1:
                sib(j).start()

    def reduce_step(s, j):
        slot = lax.rem(j, SLOTS)
        if s == 0:
            sib(j).wait_recv()
        for d in range(2):
            free(functools.partial(rs, s, d), j)
            off = sign[d] * (hn - s)
            if s == 0:
                half_send[slot, d] = mine(j, off, pair_of[d]).astype(BF)
            else:
                rs(s - 1, d, j).wait_recv()
                if s == 1:
                    full_send[slot, 0, d, :, pair_of[1 - d]] = mine(j, off, pair_of[1 - d]).astype(BF)
                    full_send[slot, 0, d, :, pair_of[d]] = (
                        mine(j, off, pair_of[d]) + half_in[j, d].astype(F32)).astype(BF)
                else:
                    full_send[slot, s - 1, d] = (mine(j, off) + full_in[j, s - 2, d].astype(F32)).astype(BF)
            rs(s, d, j).start()

    def spread(k):
        at = lax.broadcasted_iota(jnp.int32, (g, mp), 1) - lax.broadcasted_iota(jnp.int32, (g, mp), 0)
        col = jnp.sum(jnp.where(at == me * g, scr[k], 0.0), axis=1, keepdims=True)
        scale[k] = jnp.broadcast_to(col, (g, 128))

    def activate(j):
        k, chunk = where(j)

        @pl.when(j == 0)
        def _():
            tot = ss[...]
            for d in range(1, nr):
                ss_copy(d).wait_recv()
                tot = tot + ssr[d - 1]
            scr[0] = lax.rsqrt(tot / total + 1e-5)
            for i in range(1, nz):
                scale_copy(i).start()
            spread(0)

        @pl.when((chunk == 0) & (k > 0))
        def _():
            ref = scr.at[k]
            remote(ref, ref, sc_sems.at[0, k - 1], sc_sems.at[1, k - 1], {"col": plane(1)}).wait_recv()
            spread(k)
        for d in range(2):
            rs(hn - 1, d, j).wait_recv()
        val = mine(j, 0) + full_in[j, hn - 2, 0].astype(F32) + full_in[j, hn - 2, 1].astype(F32)
        val = val * scale[k][:, 0:1]
        gate, up = val[:, :hw], val[:, hw:]
        h_all[j, core, me] = (gate / (1.0 + jnp.exp(-gate)) * up).astype(BF)
        for d in range(2):
            free(functools.partial(ag, 0, d), j)
            ag(0, d, j).start()

    def gather_step(s, j):
        for d in range(2):
            ag(s - 1, d, j, True).wait_recv()
            free(functools.partial(ag, s, d), j)
            ag(s, d, j).start()

    def gather_last(j):
        for d in range(2):
            ag(hn - 1, d, j, True).wait_recv()
        free(hs, j)
        hs(j).start()

    def down(j):
        slot = lax.rem(j, 2)
        k, _ = where(j)

        @pl.when(j + 1 < items)
        def _():
            down_load(j + 1).start()
        down_load(j).wait()
        hs(j, True).wait_recv()
        tile = 256
        for t in range(feat // tile):
            cols = slice(t * tile, (t + 1) * tile)
            res = jnp.dot(h_all[j, 0].reshape(m, hw), wdn[slot, :hw, cols], preferred_element_type=F32)
            res = res + jnp.dot(h_all[j, 1].reshape(m, hw), wdn[slot, hw:, cols], preferred_element_type=F32)
            acc[k, :, cols] += res

    stages = [functools.partial(reduce_step, s) for s in range(hn)] + [activate]
    stages += [functools.partial(gather_step, s) for s in range(1, hn)] + [gather_last]
    order = [(1 + LAG * i, f) for i, f in enumerate(stages)]
    last = order[-1][0] + 1
    order += [(0, first), (last, down)]

    def c_copy(k):
        return remote(cs.at[k - 1], cr.at[k - 1], c_sems.at[0, k - 1], c_sems.at[1, k - 1],
                      {"col": plane(k)})

    @pl.loop(0, items + last)
    def _(t):
        for k in range(2, nz):
            @pl.when(t == lead + (k - 2) * chunks)
            def _():
                x_copy(k).start()
        for lag, stage in order:
            @pl.when((t >= lag) & (t - lag < items))
            def _():
                stage(t - lag)
        for k in range(1, nz):
            @pl.when(t == lead + k * chunks - 1 + last)
            def _():
                cs[k - 1] = acc[k].astype(BF)
                c_copy(k).start()

    res = acc[0]
    for k in range(1, nz):
        c_copy(k).wait_recv()
        res = res + cr[k - 1].astype(F32)
    out = res.astype(BF)
    out_ref[...] = out
    diff = out.astype(F32) - teacher_ref[map_ref[0]].astype(F32)
    sq = jnp.sum((diff * diff).reshape(m // 8, 8, feat), axis=0)
    part = sq[:, 0:128]
    for c in range(1, feat // 128):
        part = part + sq[:, c * 128:(c + 1) * 128]

    def l_copy(axis, d):
        size, at = (nr, r) if axis == "row" else (nz, z)
        src, dst = (lsum.at[0], l_row) if axis == "row" else (lsum.at[1], l_col)
        base = 0 if axis == "row" else nr - 1
        return remote(src, dst.at[d - 1], l_sems.at[0, base + d - 1], l_sems.at[1, base + d - 1],
                      {axis: lax.rem(at + d, size)})

    lsum[0] = part
    for d in range(1, nr):
        l_copy("row", d).start()
    for d in range(1, nr):
        l_copy("row", d).wait_recv()
        part = part + l_row[d - 1]
    lsum[1] = part
    for d in range(1, nz):
        l_copy("col", d).start()
    for d in range(1, nz):
        l_copy("col", d).wait_recv()
        part = part + l_col[d - 1]
    loss_ref[...] = part

    for d in range(1, nr):
        l_copy("row", d).wait_send()
        ss_copy(d).wait_send()
    for k in range(1, nz):
        l_copy("col", k).wait_send()
        x_copy(k).wait_send()
        scale_copy(k).wait_send()
        c_copy(k).wait_send()
    for i in range(SLOTS):
        j = jnp.int32(items - SLOTS + i)
        if i >= SLOTS - 2:
            sib(j).wait_send()
        for d in range(2):
            for s in range(hn):
                rs(s, d, j).wait_send()
                ag(s, d, j).wait_send()
        hs(j).wait_send()


def body(nr, nz, student_in, norm_gain, w_gate, w_up, w_down, teacher, layer_map):
    m, feat = student_in.shape
    ff = w_gate.shape[1]
    n, hn = nr // 2, nr // 4
    g = m // n
    mp = -(-m // 128) * 128
    w = next(v for v in (512, 256) if ff % v == 0)
    hw = w // 2
    chunks = ff // w
    c = nz * chunks
    lead = chunks - chunks // 3
    own = 1 + hn * LAG
    vm, dma = pltpu.VMEM, pltpu.SemaphoreType.DMA
    spec = pl.BlockSpec(memory_space=pltpu.VMEM)
    hbm = pl.BlockSpec(memory_space=pl.ANY)
    out, loss = pl.pallas_call(
        functools.partial(kernel, nr, nz, w, feat * nr, lead),
        out_shape=(jax.ShapeDtypeStruct((m, feat), BF), jax.ShapeDtypeStruct((8, 128), F32)),
        in_specs=[spec, spec, hbm, hbm, hbm, spec, pl.BlockSpec(memory_space=pltpu.SMEM)],
        out_specs=(spec, spec),
        scratch_shapes=[
            vm((nz, m, feat), BF),
            vm((1, mp), F32),
            vm((nr - 1, 1, mp), F32),
            vm((nz, 1, mp), F32),
            vm((nz, g, 128), F32),
            vm((2, 4, feat, hw), BF),
            vm((2, w, feat), BF),
            vm((own, n, g, w), BF),
            vm((2, n, g, w), BF),
            vm((c, n, g, w), BF),
            vm((SLOTS, 2, g, hw), BF),
            vm((c, 2, g, hw), BF),
            vm((SLOTS, hn - 1, 2, g, w), BF),
            vm((c, hn - 1, 2, g, w), BF),
            vm((c, 2, n, g, hw), BF),
            vm((nz, m, feat), F32),
            vm((nz - 1, m, feat), BF),
            vm((nz - 1, m, feat), BF),
            vm((2, 8, 128), F32),
            vm((nr - 1, 8, 128), F32),
            vm((nz - 1, 8, 128), F32),
            dma((2, nz - 1)),
            dma((2, 4)),
            dma((2,)),
            dma((2, nr - 1)),
            dma((2, nz - 1)),
            dma((2 + c,)),
            dma((hn, 2, SLOTS)),
            dma((hn, 2, c)),
            dma((hn, 2, SLOTS)),
            dma((hn, 2, c)),
            dma((SLOTS + c,)),
            dma((2, nz - 1)),
            dma((2, nr + nz - 2)),
        ],
        compiler_params=pltpu.CompilerParams(
            collective_id=0, has_side_effects=True, vmem_limit_bytes=67043328),
    )(student_in, norm_gain.reshape(1, feat), w_gate, w_up, w_down, teacher, layer_map)
    return out, jnp.sum(loss) / (m * nz * feat * nr)


def solution(mesh):
    placed = (
        P("col", "row"),
        P("row"),
        P("row", "col"),
        P("row", "col"),
        P("col", "row"),
        P(None, "col", "row"),
        P(),
    )
    return jax.shard_map(
        functools.partial(body, mesh.shape["row"], mesh.shape["col"]),
        mesh=mesh, in_specs=placed, out_specs=(P("col", "row"), P()), check_vma=False
    )
```

```python
import functools

import jax
import jax.numpy as jnp
from jax import lax
from jax.experimental import pallas as pl
from jax.experimental.pallas import tpu as pltpu
from jax.sharding import PartitionSpec as P

BF = jnp.bfloat16
F32 = jnp.float32
LAG = 2
SLOTS = 4
LATE = 1
TWICE = True


def kernel(nr, nz, w, count, lead, head, x_hbm, gain_ref, wg_ref, wu_ref, wd_ref, t_hbm, map_ref,
           out_hbm, loss_ref,
           x_ref, teacher_ref, out_ref, xg, ss, ssr, scr, scale, wgu, wdn, p_own, p_send, s_in, half_send, half_in,
           full_send, full_in, all_send, all_in, wlast, h_all, acc, cs, cr, lsum, l_row, l_col,
           x_sems, w_sem, wd_sem, ss_sems, sc_sems, sib_sems, rs_send, rs_recv, ag_send, ag_recv,
           hs_sems, all_rs, all_ag, wl_sem, io_sems, c_sems, l_sems):
    items = s_in.shape[0]
    n = nr // 2
    hn = n // 2
    m, feat = x_ref.shape
    io_x = pltpu.make_async_copy(x_hbm, x_ref, io_sems.at[0])
    io_t = pltpu.make_async_copy(t_hbm, teacher_ref, io_sems.at[1])
    io_out = pltpu.make_async_copy(out_ref, out_hbm, io_sems.at[2])
    io_x.start()
    mp = ss.shape[-1]
    g = m // n
    hw = w // 2
    chunks = items // nz
    r = lax.axis_index("row")
    z = lax.axis_index("col")
    core = lax.rem(r, 2)
    chip = lax.div(r, 2)
    a, b = lax.div(chip, 2), lax.rem(chip, 2)
    pos = a + b * (n - 1 - 2 * a)

    def chip_at(off):
        q = lax.rem(pos + (off % n), n)
        far = lax.div(q, hn)
        return far * (2 * (n - 1 - q) + 1) + (1 - far) * 2 * q

    me = chip_at(0)
    sibling = {"row": chip * 2 + 1 - core}
    ring = ({"row": chip_at(1) * 2 + core}, {"row": chip_at(-1) * 2 + core})
    sign = (1, -1)
    pair_of = (slice(0, hw), slice(hw, w))
    unit_of = (pl.ds(0, hw // 2), pl.ds(hw // 2, hw // 2))
    late = items - all_in.shape[0]
    inner = (nz - 1) * chunks

    def plane(k, back=False):
        if nz & (nz - 1):
            return lax.rem(z + (nz - k if back else k), nz)
        q, bit = z, 1
        while bit <= k:
            if k & bit:
                q = q + bit * (1 - 2 * lax.rem(lax.div(z, bit), 2))
            bit *= 2
        return q

    def remote(src, dst, send, recv, dev):
        return pltpu.make_async_remote_copy(
            src_ref=src, dst_ref=dst, send_sem=send, recv_sem=recv,
            device_id=dev, device_id_type=pl.DeviceIdType.MESH)

    def where(j):
        part = lax.div(j + (inner - lead), inner)
        mid = lax.rem(part, 2)
        v = j - lead + (chunks - head)
        u = j + (chunks - lead) - lax.div(part, 2) * inner
        return (mid * (1 + lax.rem(lax.div(v, chunks), nz - 1)),
                mid * lax.rem(v, chunks) + (1 - mid) * lax.rem(u, chunks))

    def begins(k):
        return lead + (0 if k == 1 else head + (k - 2) * chunks)

    def ends(k):
        return lead + (inner if k == 1 else head + (k - 1) * chunks) - 1

    def up_load(j):
        slot = lax.rem(j, 2)
        copies = []
        for part, c in enumerate((1 - core, core)):
            cols = pl.ds(pl.multiple_of(where(j)[1] * w + c * hw, hw), hw)
            for u, ref in enumerate((wg_ref, wu_ref)):
                copies.append(pltpu.make_async_copy(
                    ref.at[:, cols], wgu.at[slot, 2 * part + u], w_sem.at[slot, 2 * part + u]))
        return copies

    def down_load(j):
        slot = lax.rem(j, 2)
        return pltpu.make_async_copy(
            wd_ref.at[pl.ds(pl.multiple_of(where(j)[1] * w, w), w)], wdn.at[slot], wd_sem.at[slot])

    for c in up_load(jnp.int32(0)):
        c.start()
    down_load(jnp.int32(0)).start()
    io_t.start()

    barrier = pltpu.get_barrier_semaphore()
    for d in range(1, nr):
        pl.semaphore_signal(barrier, inc=1, device_id={"row": lax.rem(r + d, nr)},
                            device_id_type=pl.DeviceIdType.MESH)
    for d in range(1, nz):
        pl.semaphore_signal(barrier, inc=1, device_id={"col": lax.rem(z + d, nz)},
                            device_id_type=pl.DeviceIdType.MESH)

    io_x.wait()

    xf = x_ref[...].astype(F32)
    xg[0] = (xf * gain_ref[...].astype(F32)[None, :]).astype(BF)
    pl.semaphore_wait(barrier, nr - 1 + nz - 1)

    def x_copy(k, back=False):
        return remote(xg.at[0], xg.at[k], x_sems.at[0, k - 1], x_sems.at[1, k - 1],
                      {"col": plane(k, not back)})

    def x_wait(k):
        ref = xg.at[k]
        remote(ref, ref, x_sems.at[0, k - 1], x_sems.at[1, k - 1], {"col": plane(1)}).wait_recv()

    def ss_copy(d):
        return remote(ss, ssr.at[d - 1], ss_sems.at[0, d - 1], ss_sems.at[1, d - 1],
                      {"row": lax.rem(r + d, nr)})

    def scale_copy(k):
        return remote(scr.at[0], scr.at[k], sc_sems.at[0, k - 1], sc_sems.at[1, k - 1],
                      {"col": plane(k, True)})

    if nz > 1:
        x_copy(1).start()

    def squares():
        xf = x_ref[...].astype(F32)
        sq = xf * xf
        part = sq[:, 0:128]
        for c in range(1, feat // 128):
            part = part + sq[:, c * 128:(c + 1) * 128]
        part = jnp.sum(part, axis=1, keepdims=True)
        same = lax.broadcasted_iota(jnp.int32, (m, mp), 0) == lax.broadcasted_iota(jnp.int32, (m, mp), 1)
        ss[...] = jnp.sum(jnp.where(same, part, 0.0), axis=0, keepdims=True)
        for d in range(1, nr):
            ss_copy(d).start()
        acc[0] = xf

    def sib(j):
        slot = lax.rem(j, 2)
        return remote(p_send.at[slot], s_in.at[j], sib_sems.at[slot], sib_sems.at[2 + j], sibling)

    def rs(s, d, j):
        slot = lax.rem(j, SLOTS)
        if s == 0:
            src, dst = half_send.at[slot, d], half_in.at[j, d]
        else:
            src, dst = full_send.at[slot, s - 1, d], full_in.at[j, s - 1, d]
        return remote(src, dst, rs_send.at[s, d, slot], rs_recv.at[s, d, j], ring[d])

    def ag(s, d, j, got=False):
        blk = chip_at(-sign[d] * (s + 1 if got else s))
        ref = h_all.at[j, core, blk]
        if s == hn - 1:
            ref = h_all.at[j, core, blk, :, unit_of[d]]
        return remote(ref, ref, ag_send.at[s, d, lax.rem(j, SLOTS)], ag_recv.at[s, d, j], ring[d])

    def hs(j, got=False):
        ref = h_all.at[j, 1 - core if got else core]
        return remote(ref, ref, hs_sems.at[lax.rem(j, SLOTS)], hs_sems.at[SLOTS + j], sibling)

    def free(make, j, slots=SLOTS):
        @pl.when(j >= slots)
        def _():
            make(j - slots).wait_send()

    def mine(j, off, cols=slice(None)):
        q = chip_at(off)
        slot = lax.rem(j, p_own.shape[0])
        return p_own[slot, q, :, cols].astype(F32) + s_in[j, q, :, cols].astype(F32)

    def first(j):
        slot = lax.rem(j, 2)
        k, _ = where(j)

        @pl.when(j + 1 < items)
        def _():
            for c in up_load(j + 1):
                c.start()

        for i in range(1, nz):
            @pl.when(j == begins(i))
            def _():
                x_wait(i)
        for c in up_load(j):
            c.wait()
        free(sib, j, 2)
        for i in range(4):
            res = jnp.dot(xg[k], wgu[slot, i], preferred_element_type=F32).astype(BF).reshape(n, g, hw)
            if i < 2:
                p_send[slot, :, :, pair_of[i]] = res
            else:
                p_own[lax.rem(j, p_own.shape[0]), :, :, pair_of[i - 2]] = res
            if i == 1:
                sib(j).start()

    def reduce_step(s, j):
        slot = lax.rem(j, SLOTS)
        if s == 0:
            sib(j).wait_recv()
        for d in range(2):
            free(functools.partial(rs, s, d), j)
            off = sign[d] * (hn - s)
            if s == 0:
                half_send[slot, d] = mine(j, off, pair_of[d]).astype(BF)
            else:
                rs(s - 1, d, j).wait_recv()
                if s == 1:
                    full_send[slot, 0, d, :, pair_of[1 - d]] = mine(j, off, pair_of[1 - d]).astype(BF)
                    full_send[slot, 0, d, :, pair_of[d]] = (
                        mine(j, off, pair_of[d]) + half_in[j, d].astype(F32)).astype(BF)
                else:
                    full_send[slot, s - 1, d] = (mine(j, off) + full_in[j, s - 2, d].astype(F32)).astype(BF)
            rs(s, d, j).start()

    def spread(k):
        at = lax.broadcasted_iota(jnp.int32, (g, mp), 1) - lax.broadcasted_iota(jnp.int32, (g, mp), 0)
        col = jnp.sum(jnp.where(at == me * g, scr[k], 0.0), axis=1, keepdims=True)
        scale[k] = jnp.broadcast_to(col, (g, 128))

    def glu(val):
        gate, up = val[:, :hw], val[:, hw:]
        return (gate / (1.0 + jnp.exp(-gate)) * up).astype(BF)

    def activate(j):
        k, _ = where(j)

        @pl.when(j == 0)
        def _():
            tot = ss[...]
            for d in range(1, nr):
                ss_copy(d).wait_recv()
                tot = tot + ssr[d - 1]
            scr[0] = lax.rsqrt(tot / (feat * nr) + 1e-5)
            for i in range(1, nz):
                scale_copy(i).start()
            spread(0)

        for i in range(1, nz):
            @pl.when(j == begins(i))
            def _():
                ref = scr.at[i]
                remote(ref, ref, sc_sems.at[0, i - 1], sc_sems.at[1, i - 1], {"col": plane(1)}).wait_recv()
                spread(i)
        for d in range(2):
            rs(hn - 1, d, j).wait_recv()
        val = mine(j, 0) + full_in[j, hn - 2, 0].astype(F32) + full_in[j, hn - 2, 1].astype(F32)
        h_all[j, core, me] = glu(val * scale[k][:, 0:1])
        for d in range(2):
            free(functools.partial(ag, 0, d), j)
            ag(0, d, j).start()

    def gather_step(s, j):
        for d in range(2):
            ag(s - 1, d, j, True).wait_recv()
            free(functools.partial(ag, s, d), j)
            ag(s, d, j).start()

    def gather_last(j):
        for d in range(2):
            ag(hn - 1, d, j, True).wait_recv()
        free(hs, j)
        hs(j).start()

    def project(j, k, wt):
        tile = 256
        for t in range(feat // tile):
            cols = slice(t * tile, (t + 1) * tile)
            res = jnp.dot(h_all[j, 0].reshape(m, hw), wt[:hw, cols], preferred_element_type=F32)
            res = res + jnp.dot(h_all[j, 1].reshape(m, hw), wt[hw:, cols], preferred_element_type=F32)
            acc[k, :, cols] += res

    def down(j):
        slot = lax.rem(j, 2)
        k, _ = where(j)

        @pl.when(j + 1 < late)
        def _():
            down_load(j + 1).start()
        down_load(j).wait()
        hs(j, True).wait_recv()
        project(j, k, wdn.at[slot])

    stages = [functools.partial(reduce_step, s) for s in range(hn)] + [activate]
    stages += [functools.partial(gather_step, s) for s in range(1, hn)] + [gather_last]
    near = [(1 + LAG * i, f) for i, f in enumerate(stages)]
    last = near[-1][0] + 1
    order = [(0, items, 0, first), (last, late, 0, down)]
    order = [(lag, late, 0, f) for lag, f in near[::-1]] + order

    def all_rs_copy(j, off):
        i = j - late
        return remote(all_send.at[i, off - 1], all_in.at[i, off - 1], all_rs.at[0, i, off - 1], all_rs.at[1, i, off - 1],
                      {"row": chip_at(off) * 2 + core})

    def all_ag_copy(j, off, flip, got=False):
        i = j - late
        at = 2 * off + flip - 1
        src = core + flip * (1 - 2 * core)
        ref = h_all.at[j, src if got else core, chip_at(-off) if got else me]
        return remote(ref, ref, all_ag.at[0, i, at], all_ag.at[1, i, at], {"row": chip_at(off) * 2 + src})

    far_first = sorted(range(1, n), key=lambda off: -min(off, n - off))
    everyone = [(off, flip) for off in far_first for flip in range(1 + TWICE)] + [(0, 1)] * TWICE

    def late_load(j):
        i = j - late
        return pltpu.make_async_copy(
            wd_ref.at[pl.ds(pl.multiple_of(where(j)[1] * w, w), w)], wlast.at[i], wl_sem.at[i])

    def late_reduce(j):
        late_load(j).start()
        sib(j).wait_recv()
        for off in far_first:
            all_send[j - late, off - 1] = mine(j, off).astype(BF)
            all_rs_copy(j, off).start()

    def late_activate(j):
        k, _ = where(j)
        val = mine(j, 0)
        for off in range(1, n):
            all_rs_copy(j, off).wait_recv()
            val = val + all_in[j - late, off - 1].astype(F32)
        h_all[j, core, me] = glu(val * scale[k][:, 0:1])
        for off, flip in everyone:
            all_ag_copy(j, off, flip).start()

    def late_pass(j):
        for off, flip in everyone:
            all_ag_copy(j, off, flip, True).wait_recv()
        if not TWICE:
            free(hs, j)
            hs(j).start()

    def late_down(j):
        late_load(j).wait()
        if not TWICE:
            hs(j, True).wait_recv()
        project(j, where(j)[0], wlast.at[j - late])

    tail = [(1, late_reduce), (1 + LAG, late_activate), (1 + 2 * LAG, late_pass), (2 + 2 * LAG, late_down)]
    order += [(lag, items, late, f) for lag, f in tail[::-1]]
    steps = max(last + late, tail[-1][0] + items)

    def c_copy(k):
        return remote(cs.at[k - 1], cr.at[k - 1], c_sems.at[0, k - 1], c_sems.at[1, k - 1],
                      {"col": plane(k)})

    @pl.loop(0, steps)
    def _(t):
        for k in range(2, nz):
            @pl.when(t == begins(k - 1) )
            def _():
                x_copy(k).start()
        @pl.when(t == steps - 2)
        def _():
            for k in range(2, nz):
                c_copy(k).wait_recv()
                acc[0] += cr[k - 1].astype(F32)
        for lag, stop, start, stage in order:
            @pl.when((t >= start + lag) & (t - lag < stop))
            def _():
                stage(t - lag)

        @pl.when(t == 0)
        def _():
            squares()
        for k in range(1, nz):
            @pl.when(t == begins(k))
            def _():
                acc[k] = jnp.zeros_like(acc[k])

            @pl.when(t == ends(k) + last)
            def _():
                cs[k - 1] = acc[k].astype(BF)
                c_copy(k).start()

    res = acc[0]
    if nz > 1:
        c_copy(1).wait_recv()
        res = res + cr[0].astype(F32)
    out = res.astype(BF)
    out_ref[...] = out
    io_out.start()
    io_t.wait()
    diff = out.astype(F32) - teacher_ref[map_ref[0]].astype(F32)
    sq = jnp.sum((diff * diff).reshape(m // 8, 8, feat), axis=0)
    part = sq[:, 0:128]
    for c in range(1, feat // 128):
        part = part + sq[:, c * 128:(c + 1) * 128]

    def l_copy(axis, d):
        size, at = (nr, r) if axis == "row" else (nz, z)
        src, dst = (lsum.at[0], l_row) if axis == "row" else (lsum.at[1], l_col)
        base = 0 if axis == "row" else nr - 1
        return remote(src, dst.at[d - 1], l_sems.at[0, base + d - 1], l_sems.at[1, base + d - 1],
                      {axis: lax.rem(at + d, size)})

    lsum[0] = part
    for d in range(1, nr):
        l_copy("row", d).start()
    for d in range(1, nr):
        l_copy("row", d).wait_recv()
        part = part + l_row[d - 1]
    lsum[1] = part
    for d in range(1, nz):
        l_copy("col", d).start()
    for d in range(1, nz):
        l_copy("col", d).wait_recv()
        part = part + l_col[d - 1]
    loss_ref[0, 0] = jnp.sum(part) / count

    for d in range(1, nr):
        l_copy("row", d).wait_send()
        ss_copy(d).wait_send()
    for k in range(1, nz):
        l_copy("col", k).wait_send()
        x_copy(k).wait_send()
        scale_copy(k).wait_send()
        c_copy(k).wait_send()
    for i in range(2):
        sib(jnp.int32(items - 2 + i)).wait_send()
    for i in range(items - late):
        j = jnp.int32(late + i)
        for off in range(1, n):
            all_rs_copy(j, off).wait_send()
        for off, flip in everyone:
            all_ag_copy(j, off, flip).wait_send()
    for i in range(SLOTS):
        j = jnp.int32(late - SLOTS + i)
        for d in range(2):
            for s in range(hn):
                rs(s, d, j).wait_send()
                ag(s, d, j).wait_send()
        hs(jnp.int32((late if TWICE else items) - SLOTS + i)).wait_send()
    io_out.wait()


def body(nr, nz, student_in, norm_gain, w_gate, w_up, w_down, teacher, layer_map):
    m, feat = student_in.shape
    ff = w_gate.shape[1]
    n, hn = nr // 2, nr // 4
    g = m // n
    mp = -(-m // 128) * 128
    w = next(v for v in (512, 256) if ff % v == 0)
    hw = w // 2
    chunks = ff // w
    c = nz * chunks
    lead = chunks // 2
    head = chunks - chunks // 3 - 1
    own = 1 + hn * LAG
    vm, dma = pltpu.VMEM, pltpu.SemaphoreType.DMA
    spec = pl.BlockSpec(memory_space=pltpu.VMEM)
    smem = pl.BlockSpec(memory_space=pltpu.SMEM)
    hbm = pl.BlockSpec(memory_space=pl.ANY)
    out, loss = pl.pallas_call(
        functools.partial(kernel, nr, nz, w, m * nz * feat * nr, lead, head),
        out_shape=(jax.ShapeDtypeStruct((m, feat), BF), jax.ShapeDtypeStruct((1, 1), F32)),
        in_specs=[hbm, spec, hbm, hbm, hbm, hbm, smem],
        out_specs=(hbm, smem),
        scratch_shapes=[
            vm((m, feat), BF),
            vm(teacher.shape, BF),
            vm((m, feat), BF),
            vm((nz, m, feat), BF),
            vm((1, mp), F32),
            vm((nr - 1, 1, mp), F32),
            vm((nz, 1, mp), F32),
            vm((nz, g, 128), F32),
            vm((2, 4, feat, hw), BF),
            vm((2, w, feat), BF),
            vm((own, n, g, w), BF),
            vm((2, n, g, w), BF),
            vm((c, n, g, w), BF),
            vm((SLOTS, 2, g, hw), BF),
            vm((c, 2, g, hw), BF),
            vm((SLOTS, hn - 1, 2, g, w), BF),
            vm((c, hn - 1, 2, g, w), BF),
            vm((LATE, n - 1, g, w), BF),
            vm((LATE, n - 1, g, w), BF),
            vm((LATE, w, feat), BF),
            vm((c, 2, n, g, hw), BF),
            vm((nz, m, feat), F32),
            vm((nz - 1, m, feat), BF),
            vm((nz - 1, m, feat), BF),
            vm((2, 8, 128), F32),
            vm((nr - 1, 8, 128), F32),
            vm((nz - 1, 8, 128), F32),
            dma((2, nz - 1)),
            dma((2, 4)),
            dma((2,)),
            dma((2, nr - 1)),
            dma((2, nz - 1)),
            dma((2 + c,)),
            dma((hn, 2, SLOTS)),
            dma((hn, 2, c)),
            dma((hn, 2, SLOTS)),
            dma((hn, 2, c)),
            dma((SLOTS + c,)),
            dma((2, LATE, n - 1)),
            dma((2, LATE, nr - 1)),
            dma((LATE,)),
            dma((3,)),
            dma((2, nz - 1)),
            dma((2, nr + nz - 2)),
        ],
        compiler_params=pltpu.CompilerParams(
            collective_id=0, has_side_effects=True, vmem_limit_bytes=67043328),
    )(student_in, norm_gain, w_gate, w_up, w_down, teacher, layer_map)
    return out, loss.reshape(())


def solution(mesh):
    placed = (
        P("col", "row"),
        P("row"),
        P("row", "col"),
        P("row", "col"),
        P("col", "row"),
        P(None, "col", "row"),
        P(),
    )
    return jax.shard_map(
        functools.partial(body, mesh.shape["row"], mesh.shape["col"]),
        mesh=mesh, in_specs=placed, out_specs=(P("col", "row"), P()), check_vma=False
    )
```

```python
import functools

import jax
import jax.numpy as jnp
from jax import lax
from jax.experimental import pallas as pl
from jax.experimental.pallas import tpu as pltpu
from jax.sharding import PartitionSpec as P

BF = jnp.bfloat16
F32 = jnp.float32
LAG = 2
SLOTS = 4
RING = 4 * LAG
LATE = 1


def kernel(nr, nz, w, count, lead, head, x_hbm, gain_ref, wg_ref, wu_ref, wd_ref, t_hbm, map_ref,
           out_hbm, loss_ref,
           x_ref, teacher_ref, out_ref, xg, ss, ssr, scr, scale, wgu, wdn, p_own, p_send, s_in, half_send, half_in,
           full_send, full_in, all_send, all_in, wlast, h_all, acc, cs, cr, lsum, l_row, l_col,
           x_sems, w_sem, wd_sem, ss_sems, sc_sems, sib_sems, rs_send, rs_recv, ag_send, ag_recv,
           hs_sems, all_rs, all_ag, wl_sem, io_sems, c_sems, l_sems):
    items = s_in.shape[0]
    n = nr // 2
    hn = n // 2
    m, feat = x_ref.shape
    io_x = pltpu.make_async_copy(x_hbm, x_ref, io_sems.at[0])
    io_t = pltpu.make_async_copy(t_hbm, teacher_ref, io_sems.at[1])
    io_out = pltpu.make_async_copy(out_ref, out_hbm, io_sems.at[2])
    io_x.start()
    mp = ss.shape[-1]
    g = m // n
    hw = w // 2
    chunks = items // nz
    r = lax.axis_index("row")
    z = lax.axis_index("col")
    core = lax.rem(r, 2)
    chip = lax.div(r, 2)
    a, b = lax.div(chip, 2), lax.rem(chip, 2)
    pos = a + b * (n - 1 - 2 * a)

    def chip_at(off):
        q = lax.rem(pos + (off % n), n)
        far = lax.div(q, hn)
        return far * (2 * (n - 1 - q) + 1) + (1 - far) * 2 * q

    me = chip_at(0)
    sibling = {"row": chip * 2 + 1 - core}
    ring = ({"row": chip_at(1) * 2 + core}, {"row": chip_at(-1) * 2 + core})
    sign = (1, -1)
    pair_of = (slice(0, hw), slice(hw, w))
    unit_of = (pl.ds(0, hw // 2), pl.ds(hw // 2, hw // 2))
    late = items - all_in.shape[0]
    inner = (nz - 1) * chunks

    def plane(k, back=False):
        if nz & (nz - 1):
            return lax.rem(z + (nz - k if back else k), nz)
        q, bit = z, 1
        while bit <= k:
            if k & bit:
                q = q + bit * (1 - 2 * lax.rem(lax.div(z, bit), 2))
            bit *= 2
        return q

    def remote(src, dst, send, recv, dev):
        return pltpu.make_async_remote_copy(
            src_ref=src, dst_ref=dst, send_sem=send, recv_sem=recv,
            device_id=dev, device_id_type=pl.DeviceIdType.MESH)

    def where(j):
        part = lax.div(j + (inner - lead), inner)
        mid = lax.rem(part, 2)
        v = j - lead + (chunks - head)
        u = j + (chunks - lead) - lax.div(part, 2) * inner
        return (mid * (1 + lax.rem(lax.div(v, chunks), nz - 1)),
                mid * lax.rem(v, chunks) + (1 - mid) * lax.rem(u, chunks))

    def begins(k):
        return lead + (0 if k == 1 else head + (k - 2) * chunks)

    def ends(k):
        return lead + (inner if k == 1 else head + (k - 1) * chunks) - 1

    def up_load(j):
        slot = lax.rem(j, 2)
        copies = []
        for part, c in enumerate((1 - core, core)):
            cols = pl.ds(pl.multiple_of(where(j)[1] * w + c * hw, hw), hw)
            for u, ref in enumerate((wg_ref, wu_ref)):
                copies.append(pltpu.make_async_copy(
                    ref.at[:, cols], wgu.at[slot, 2 * part + u], w_sem.at[slot, 2 * part + u]))
        return copies

    def down_load(j):
        slot = lax.rem(j, 2)
        return pltpu.make_async_copy(
            wd_ref.at[pl.ds(pl.multiple_of(where(j)[1] * w, w), w)], wdn.at[slot], wd_sem.at[slot])

    for c in up_load(jnp.int32(0)):
        c.start()
    down_load(jnp.int32(0)).start()
    io_t.start()

    barrier = pltpu.get_barrier_semaphore()
    for d in range(1, nr):
        pl.semaphore_signal(barrier, inc=1, device_id={"row": lax.rem(r + d, nr)},
                            device_id_type=pl.DeviceIdType.MESH)
    for d in range(1, nz):
        pl.semaphore_signal(barrier, inc=1, device_id={"col": lax.rem(z + d, nz)},
                            device_id_type=pl.DeviceIdType.MESH)

    io_x.wait()

    xf = x_ref[...].astype(F32)
    xg[0] = (xf * gain_ref[...].astype(F32)[None, :]).astype(BF)
    pl.semaphore_wait(barrier, nr - 1 + nz - 1)

    def x_copy(k, back=False):
        return remote(xg.at[0], xg.at[k], x_sems.at[0, k - 1], x_sems.at[1, k - 1],
                      {"col": plane(k, not back)})

    def x_wait(k):
        ref = xg.at[k]
        remote(ref, ref, x_sems.at[0, k - 1], x_sems.at[1, k - 1], {"col": plane(1)}).wait_recv()

    def ss_copy(d):
        return remote(ss, ssr.at[d - 1], ss_sems.at[0, d - 1], ss_sems.at[1, d - 1],
                      {"row": lax.rem(r + d, nr)})

    def scale_copy(k):
        return remote(scr.at[0], scr.at[k], sc_sems.at[0, k - 1], sc_sems.at[1, k - 1],
                      {"col": plane(k, True)})

    if nz > 1:
        x_copy(1).start()

    def squares():
        xf = x_ref[...].astype(F32)
        sq = xf * xf
        part = sq[:, 0:128]
        for c in range(1, feat // 128):
            part = part + sq[:, c * 128:(c + 1) * 128]
        part = jnp.sum(part, axis=1, keepdims=True)
        same = lax.broadcasted_iota(jnp.int32, (m, mp), 0) == lax.broadcasted_iota(jnp.int32, (m, mp), 1)
        ss[...] = jnp.sum(jnp.where(same, part, 0.0), axis=0, keepdims=True)
        for d in range(1, nr):
            ss_copy(d).start()
        acc[0] = xf

    def sib(j):
        slot = lax.rem(j, 2)
        return remote(p_send.at[slot], s_in.at[j], sib_sems.at[slot], sib_sems.at[2 + lax.rem(j, RING)], sibling)

    def rs(s, d, j):
        slot = lax.rem(j, SLOTS)
        if s == 0:
            src, dst = half_send.at[slot, d], half_in.at[j, d]
        else:
            src, dst = full_send.at[slot, s - 1, d], full_in.at[j, s - 1, d]
        return remote(src, dst, rs_send.at[s, d, slot], rs_recv.at[s, d, lax.rem(j, RING)], ring[d])

    def ag(s, d, j, got=False):
        blk = chip_at(-sign[d] * (s + 1 if got else s))
        ref = h_all.at[j, core, blk]
        if s == hn - 1:
            ref = h_all.at[j, core, blk, :, unit_of[d]]
        return remote(ref, ref, ag_send.at[s, d, lax.rem(j, SLOTS)], ag_recv.at[s, d, lax.rem(j, RING)], ring[d])

    def hs(j, got=False):
        ref = h_all.at[j, 1 - core if got else core]
        return remote(ref, ref, hs_sems.at[lax.rem(j, SLOTS)], hs_sems.at[SLOTS + lax.rem(j, RING)], sibling)

    def free(make, j, slots=SLOTS):
        @pl.when(j >= slots)
        def _():
            make(j - slots).wait_send()

    def mine(j, off, cols=slice(None)):
        q = chip_at(off)
        slot = lax.rem(j, p_own.shape[0])
        return p_own[slot, q, :, cols].astype(F32) + s_in[j, q, :, cols].astype(F32)

    def first(j):
        slot = lax.rem(j, 2)
        k, _ = where(j)

        @pl.when(j + 1 < items)
        def _():
            for c in up_load(j + 1):
                c.start()

        for i in range(1, nz):
            @pl.when(j == begins(i))
            def _():
                x_wait(i)
        for c in up_load(j):
            c.wait()
        free(sib, j, 2)
        for i in range(4):
            res = jnp.dot(xg[k], wgu[slot, i], preferred_element_type=F32).astype(BF).reshape(n, g, hw)
            if i < 2:
                p_send[slot, :, :, pair_of[i]] = res
            else:
                p_own[lax.rem(j, p_own.shape[0]), :, :, pair_of[i - 2]] = res
            if i == 1:
                sib(j).start()

    def reduce_step(s, j):
        slot = lax.rem(j, SLOTS)
        if s == 0:
            sib(j).wait_recv()
        for d in range(2):
            free(functools.partial(rs, s, d), j)
            off = sign[d] * (hn - s)
            if s == 0:
                half_send[slot, d] = mine(j, off, pair_of[d]).astype(BF)
            else:
                rs(s - 1, d, j).wait_recv()
                if s == 1:
                    full_send[slot, 0, d, :, pair_of[1 - d]] = mine(j, off, pair_of[1 - d]).astype(BF)
                    full_send[slot, 0, d, :, pair_of[d]] = (
                        mine(j, off, pair_of[d]) + half_in[j, d].astype(F32)).astype(BF)
                else:
                    full_send[slot, s - 1, d] = (mine(j, off) + full_in[j, s - 2, d].astype(F32)).astype(BF)
            rs(s, d, j).start()

    def spread(k):
        at = lax.broadcasted_iota(jnp.int32, (g, mp), 1) - lax.broadcasted_iota(jnp.int32, (g, mp), 0)
        col = jnp.sum(jnp.where(at == me * g, scr[k], 0.0), axis=1, keepdims=True)
        scale[k] = jnp.broadcast_to(col, (g, 128))

    def glu(val):
        gate, up = val[:, :hw], val[:, hw:]
        return (gate / (1.0 + jnp.exp(-gate)) * up).astype(BF)

    def activate(j):
        k, _ = where(j)

        @pl.when(j == 0)
        def _():
            tot = ss[...]
            for d in range(1, nr):
                ss_copy(d).wait_recv()
                tot = tot + ssr[d - 1]
            scr[0] = lax.rsqrt(tot / (feat * nr) + 1e-5)
            for i in range(1, nz):
                scale_copy(i).start()
            spread(0)

        for i in range(1, nz):
            @pl.when(j == begins(i))
            def _():
                ref = scr.at[i]
                remote(ref, ref, sc_sems.at[0, i - 1], sc_sems.at[1, i - 1], {"col": plane(1)}).wait_recv()
                spread(i)
        for d in range(2):
            rs(hn - 1, d, j).wait_recv()
        val = mine(j, 0) + full_in[j, hn - 2, 0].astype(F32) + full_in[j, hn - 2, 1].astype(F32)
        h_all[j, core, me] = glu(val * scale[k][:, 0:1])
        for d in range(2):
            free(functools.partial(ag, 0, d), j)
            ag(0, d, j).start()

    def gather_step(s, j):
        for d in range(2):
            ag(s - 1, d, j, True).wait_recv()
            free(functools.partial(ag, s, d), j)
            ag(s, d, j).start()

    def gather_last(j):
        for d in range(2):
            ag(hn - 1, d, j, True).wait_recv()
        free(hs, j)
        hs(j).start()

    def project(j, k, wt):
        tile = 256
        for t in range(feat // tile):
            cols = slice(t * tile, (t + 1) * tile)
            res = jnp.dot(h_all[j, 0].reshape(m, hw), wt[:hw, cols], preferred_element_type=F32)
            res = res + jnp.dot(h_all[j, 1].reshape(m, hw), wt[hw:, cols], preferred_element_type=F32)
            acc[k, :, cols] += res

    def down(j):
        slot = lax.rem(j, 2)
        k, _ = where(j)

        @pl.when(j + 1 < late)
        def _():
            down_load(j + 1).start()
        down_load(j).wait()
        hs(j, True).wait_recv()
        project(j, k, wdn.at[slot])

    stages = [functools.partial(reduce_step, s) for s in range(hn)] + [activate]
    stages += [functools.partial(gather_step, s) for s in range(1, hn)] + [gather_last]
    near = [(1 + LAG * i, f) for i, f in enumerate(stages)]
    last = near[-1][0] + 1
    order = [(0, items, 0, first), (last, late, 0, down)]
    order = [(lag, late, 0, f) for lag, f in near[::-1]] + order

    def all_rs_copy(j, off):
        i = j - late
        return remote(all_send.at[i, off - 1], all_in.at[i, off - 1], all_rs.at[0, i, off - 1], all_rs.at[1, i, off - 1],
                      {"row": chip_at(off) * 2 + core})

    def all_ag_copy(j, off, flip, got=False):
        i = j - late
        at = 2 * off + flip - 1
        src = core + flip * (1 - 2 * core)
        ref = h_all.at[j, src if got else core, chip_at(-off) if got else me]
        return remote(ref, ref, all_ag.at[0, i, at], all_ag.at[1, i, at], {"row": chip_at(off) * 2 + src})

    far_first = sorted(range(1, n), key=lambda off: -min(off, n - off))
    everyone = [(off, flip) for off in far_first for flip in range(2)] + [(0, 1)]

    def late_load(j):
        i = j - late
        return pltpu.make_async_copy(
            wd_ref.at[pl.ds(pl.multiple_of(where(j)[1] * w, w), w)], wlast.at[i], wl_sem.at[i])

    def late_reduce(j):
        late_load(j).start()
        sib(j).wait_recv()
        for off in far_first:
            all_send[j - late, off - 1] = mine(j, off).astype(BF)
            all_rs_copy(j, off).start()

    def late_activate(j):
        k, _ = where(j)
        val = mine(j, 0)
        for off in range(1, n):
            all_rs_copy(j, off).wait_recv()
            val = val + all_in[j - late, off - 1].astype(F32)
        h_all[j, core, me] = glu(val * scale[k][:, 0:1])
        for off, flip in everyone:
            all_ag_copy(j, off, flip).start()

    def late_down(j):
        late_load(j).wait()
        for off, flip in everyone:
            all_ag_copy(j, off, flip, True).wait_recv()
        project(j, where(j)[0], wlast.at[j - late])

    tail = [(1, late_reduce), (1 + LAG, late_activate), (1 + 2 * LAG, late_down)]
    order += [(lag, items, late, f) for lag, f in tail[::-1]]
    steps = max(last + late, tail[-1][0] + items)

    def c_copy(k):
        return remote(cs.at[k - 1], cr.at[k - 1], c_sems.at[0, k - 1], c_sems.at[1, k - 1],
                      {"col": plane(k)})

    @pl.loop(0, steps)
    def _(t):
        for k in range(2, nz):
            @pl.when(t == begins(k - 1) )
            def _():
                x_copy(k).start()
        @pl.when(t == steps - 2)
        def _():
            for k in range(2, nz):
                c_copy(k).wait_recv()
                acc[0] += cr[k - 1].astype(F32)
        for lag, stop, start, stage in order:
            @pl.when((t >= start + lag) & (t - lag < stop))
            def _():
                stage(t - lag)

        @pl.when(t == 0)
        def _():
            squares()
        for k in range(1, nz):
            @pl.when(t == begins(k))
            def _():
                acc[k] = jnp.zeros_like(acc[k])

            @pl.when(t == ends(k) + last)
            def _():
                cs[k - 1] = acc[k].astype(BF)
                c_copy(k).start()

    res = acc[0]
    if nz > 1:
        c_copy(1).wait_recv()
        res = res + cr[0].astype(F32)
    out = res.astype(BF)
    out_ref[...] = out
    io_out.start()
    io_t.wait()
    diff = out.astype(F32) - teacher_ref[map_ref[0]].astype(F32)
    sq = jnp.sum((diff * diff).reshape(m // 8, 8, feat), axis=0)
    part = sq[:, 0:128]
    for c in range(1, feat // 128):
        part = part + sq[:, c * 128:(c + 1) * 128]

    def l_copy(axis, d):
        size, at = (nr, r) if axis == "row" else (nz, z)
        src, dst = (lsum.at[0], l_row) if axis == "row" else (lsum.at[1], l_col)
        base = 0 if axis == "row" else nr - 1
        return remote(src, dst.at[d - 1], l_sems.at[0, base + d - 1], l_sems.at[1, base + d - 1],
                      {axis: lax.rem(at + d, size)})

    lsum[0] = part
    for d in range(1, nr):
        l_copy("row", d).start()
    for d in range(1, nr):
        l_copy("row", d).wait_recv()
        part = part + l_row[d - 1]
    lsum[1] = part
    for d in range(1, nz):
        l_copy("col", d).start()
    for d in range(1, nz):
        l_copy("col", d).wait_recv()
        part = part + l_col[d - 1]
    loss_ref[0, 0] = jnp.sum(part) / count

    for d in range(1, nr):
        l_copy("row", d).wait_send()
        ss_copy(d).wait_send()
    for k in range(1, nz):
        l_copy("col", k).wait_send()
        x_copy(k).wait_send()
        scale_copy(k).wait_send()
        c_copy(k).wait_send()
    for i in range(2):
        sib(jnp.int32(items - 2 + i)).wait_send()
    for i in range(items - late):
        j = jnp.int32(late + i)
        for off in range(1, n):
            all_rs_copy(j, off).wait_send()
        for off, flip in everyone:
            all_ag_copy(j, off, flip).wait_send()
    for i in range(SLOTS):
        j = jnp.int32(late - SLOTS + i)
        for d in range(2):
            for s in range(hn):
                rs(s, d, j).wait_send()
                ag(s, d, j).wait_send()
        hs(j).wait_send()
    io_out.wait()


def body(nr, nz, student_in, norm_gain, w_gate, w_up, w_down, teacher, layer_map):
    m, feat = student_in.shape
    ff = w_gate.shape[1]
    n, hn = nr // 2, nr // 4
    g = m // n
    mp = -(-m // 128) * 128
    w = next(v for v in (512, 256) if ff % v == 0)
    hw = w // 2
    chunks = ff // w
    c = nz * chunks
    lead = chunks // 2
    head = chunks - chunks // 3 - 1
    own = 1 + hn * LAG
    vm, dma = pltpu.VMEM, pltpu.SemaphoreType.DMA
    spec = pl.BlockSpec(memory_space=pltpu.VMEM)
    smem = pl.BlockSpec(memory_space=pltpu.SMEM)
    hbm = pl.BlockSpec(memory_space=pl.ANY)
    out, loss = pl.pallas_call(
        functools.partial(kernel, nr, nz, w, m * nz * feat * nr, lead, head),
        out_shape=(jax.ShapeDtypeStruct((m, feat), BF), jax.ShapeDtypeStruct((1, 1), F32)),
        in_specs=[hbm, spec, hbm, hbm, hbm, hbm, smem],
        out_specs=(hbm, smem),
        scratch_shapes=[
            vm((m, feat), BF),
            vm(teacher.shape, BF),
            vm((m, feat), BF),
            vm((nz, m, feat), BF),
            vm((1, mp), F32),
            vm((nr - 1, 1, mp), F32),
            vm((nz, 1, mp), F32),
            vm((nz, g, 128), F32),
            vm((2, 4, feat, hw), BF),
            vm((2, w, feat), BF),
            vm((own, n, g, w), BF),
            vm((2, n, g, w), BF),
            vm((c, n, g, w), BF),
            vm((SLOTS, 2, g, hw), BF),
            vm((c, 2, g, hw), BF),
            vm((SLOTS, hn - 1, 2, g, w), BF),
            vm((c, hn - 1, 2, g, w), BF),
            vm((LATE, n - 1, g, w), BF),
            vm((LATE, n - 1, g, w), BF),
            vm((LATE, w, feat), BF),
            vm((c, 2, n, g, hw), BF),
            vm((nz, m, feat), F32),
            vm((nz - 1, m, feat), BF),
            vm((nz - 1, m, feat), BF),
            vm((2, 8, 128), F32),
            vm((nr - 1, 8, 128), F32),
            vm((nz - 1, 8, 128), F32),
            dma((2, nz - 1)),
            dma((2, 4)),
            dma((2,)),
            dma((2, nr - 1)),
            dma((2, nz - 1)),
            dma((2 + RING,)),
            dma((hn, 2, SLOTS)),
            dma((hn, 2, RING)),
            dma((hn, 2, SLOTS)),
            dma((hn, 2, RING)),
            dma((SLOTS + RING,)),
            dma((2, LATE, n - 1)),
            dma((2, LATE, nr - 1)),
            dma((LATE,)),
            dma((3,)),
            dma((2, nz - 1)),
            dma((2, nr + nz - 2)),
        ],
        compiler_params=pltpu.CompilerParams(
            collective_id=0, has_side_effects=True, vmem_limit_bytes=67043328),
    )(student_in, norm_gain, w_gate, w_up, w_down, teacher, layer_map)
    return out, loss.reshape(())


def solution(mesh):
    placed = (
        P("col", "row"),
        P("row"),
        P("row", "col"),
        P("row", "col"),
        P("col", "row"),
        P(None, "col", "row"),
        P(),
    )
    return jax.shard_map(
        functools.partial(body, mesh.shape["row"], mesh.shape["col"]),
        mesh=mesh, in_specs=placed, out_specs=(P("col", "row"), P()), check_vma=False
    )
```

```python
import functools

import jax
import jax.numpy as jnp
from jax import lax
from jax.experimental import pallas as pl
from jax.experimental.pallas import tpu as pltpu
from jax.sharding import PartitionSpec as P

BF = jnp.bfloat16
F32 = jnp.float32
LAG = 2
SLOTS = 4
RING = 3 * LAG
LATE = 1


def kernel(nr, nz, w, count, lead, head, x_hbm, gain_ref, wg_ref, wu_ref, wd_ref, t_hbm, map_ref,
           out_hbm, loss_ref,
           x_ref, teacher_ref, out_ref, xg, ss, ssr, scr, scale, wgu, wdn, p_own, p_send, s_in, half_send, half_in,
           full_send, full_in, all_send, all_in, wlast, h_all, acc, cs, cr, lsum, l_row, l_col,
           x_sems, w_sem, wd_sem, ss_sems, sc_sems, sib_sems, rs_send, rs_recv, ag_send, ag_recv,
           hs_sems, all_rs, all_ag, wl_sem, io_sems, c_sems):
    items = s_in.shape[0]
    n = nr // 2
    hn = n // 2
    m, feat = x_ref.shape
    io_x = pltpu.make_async_copy(x_hbm, x_ref, io_sems.at[0])
    io_t = pltpu.make_async_copy(t_hbm, teacher_ref, io_sems.at[1])
    io_out = pltpu.make_async_copy(out_ref, out_hbm, io_sems.at[2])
    io_x.start()
    mp = ss.shape[-1]
    g = m // n
    hw = w // 2
    chunks = items // nz
    r = lax.axis_index("row")
    z = lax.axis_index("col")
    core = lax.rem(r, 2)
    chip = lax.div(r, 2)
    a, b = lax.div(chip, 2), lax.rem(chip, 2)
    pos = a + b * (n - 1 - 2 * a)

    def chip_at(off):
        q = lax.rem(pos + (off % n), n)
        far = lax.div(q, hn)
        return far * (2 * (n - 1 - q) + 1) + (1 - far) * 2 * q

    me = chip_at(0)
    sibling = {"row": chip * 2 + 1 - core}
    ring = ({"row": chip_at(1) * 2 + core}, {"row": chip_at(-1) * 2 + core})
    sign = (1, -1)
    pair_of = (slice(0, hw), slice(hw, w))
    unit_of = (pl.ds(0, hw // 2), pl.ds(hw // 2, hw // 2))
    late = items - all_in.shape[0]
    inner = (nz - 1) * chunks

    def plane(k, back=False):
        if nz & (nz - 1):
            return lax.rem(z + (nz - k if back else k), nz)
        q, bit = z, 1
        while bit <= k:
            if k & bit:
                q = q + bit * (1 - 2 * lax.rem(lax.div(z, bit), 2))
            bit *= 2
        return q

    def remote(src, dst, send, recv, dev):
        return pltpu.make_async_remote_copy(
            src_ref=src, dst_ref=dst, send_sem=send, recv_sem=recv,
            device_id=dev, device_id_type=pl.DeviceIdType.MESH)

    def where(j):
        part = lax.div(j + (inner - lead), inner)
        mid = lax.rem(part, 2)
        v = j - lead + (chunks - head)
        u = j + (chunks - lead) - lax.div(part, 2) * inner
        return (mid * (1 + lax.rem(lax.div(v, chunks), nz - 1)),
                mid * lax.rem(v, chunks) + (1 - mid) * lax.rem(u, chunks))

    def begins(k):
        return lead + (0 if k == 1 else head + (k - 2) * chunks)

    def ends(k):
        return lead + (inner if k == 1 else head + (k - 1) * chunks) - 1

    def up_load(j):
        slot = lax.rem(j, 2)
        copies = []
        cols = pl.ds(pl.multiple_of(where(j)[1] * w, w), w)
        for u, ref in enumerate((wg_ref, wu_ref)):
            copies.append(pltpu.make_async_copy(ref.at[:, cols], wgu.at[slot, u], w_sem.at[slot, u]))
        return copies

    def down_load(j):
        slot = lax.rem(j, 2)
        return pltpu.make_async_copy(
            wd_ref.at[pl.ds(pl.multiple_of(where(j)[1] * w, w), w)], wdn.at[slot], wd_sem.at[slot])

    for c in up_load(jnp.int32(0)):
        c.start()
    down_load(jnp.int32(0)).start()
    io_t.start()

    barrier = pltpu.get_barrier_semaphore()
    for d in range(1, nr):
        pl.semaphore_signal(barrier, inc=1, device_id={"row": lax.rem(r + d, nr)},
                            device_id_type=pl.DeviceIdType.MESH)
    for d in range(1, nz):
        pl.semaphore_signal(barrier, inc=1, device_id={"col": lax.rem(z + d, nz)},
                            device_id_type=pl.DeviceIdType.MESH)

    io_x.wait()

    xf = x_ref[...].astype(F32)
    xg[0] = (xf * gain_ref[...].astype(F32)[None, :]).astype(BF)
    pl.semaphore_wait(barrier, nr - 1 + nz - 1)

    def x_copy(k, back=False):
        return remote(xg.at[0], xg.at[k], x_sems.at[0, k - 1], x_sems.at[1, k - 1],
                      {"col": plane(k, not back)})

    def x_wait(k):
        ref = xg.at[k]
        remote(ref, ref, x_sems.at[0, k - 1], x_sems.at[1, k - 1], {"col": plane(1)}).wait_recv()

    def ss_copy(d):
        return remote(ss, ssr.at[d - 1], ss_sems.at[0, d - 1], ss_sems.at[1, d - 1],
                      {"row": lax.rem(r + d, nr)})

    def scale_copy(k):
        return remote(scr.at[0], scr.at[k], sc_sems.at[0, k - 1], sc_sems.at[1, k - 1],
                      {"col": plane(k, True)})

    if nz > 1:
        x_copy(1).start()

    def squares():
        xf = x_ref[...].astype(F32)
        sq = xf * xf
        part = sq[:, 0:128]
        for c in range(1, feat // 128):
            part = part + sq[:, c * 128:(c + 1) * 128]
        part = jnp.sum(part, axis=1, keepdims=True)
        same = lax.broadcasted_iota(jnp.int32, (m, mp), 0) == lax.broadcasted_iota(jnp.int32, (m, mp), 1)
        ss[...] = jnp.sum(jnp.where(same, part, 0.0), axis=0, keepdims=True)
        for d in range(1, nr):
            ss_copy(d).start()
        acc[0] = xf

    def sib(j):
        slot = lax.rem(j, 2)
        return remote(p_send.at[slot], s_in.at[j], sib_sems.at[slot], sib_sems.at[2 + lax.rem(j, RING)], sibling)

    def rs(s, d, j):
        slot = lax.rem(j, SLOTS)
        if s == 0:
            src, dst = half_send.at[slot, d], half_in.at[j, d]
        else:
            src, dst = full_send.at[slot, s - 1, d], full_in.at[j, s - 1, d]
        return remote(src, dst, rs_send.at[s, d, slot], rs_recv.at[s, d, lax.rem(j, RING)], ring[d])

    def ag(s, d, j, got=False):
        blk = chip_at(-sign[d] * (s + 1 if got else s))
        ref = h_all.at[j, core, blk]
        if s == hn - 1:
            ref = h_all.at[j, core, blk, :, unit_of[d]]
        return remote(ref, ref, ag_send.at[s, d, lax.rem(j, SLOTS)], ag_recv.at[s, d, lax.rem(j, RING)], ring[d])

    def hs(j, got=False):
        ref = h_all.at[j, 1 - core if got else core]
        return remote(ref, ref, hs_sems.at[lax.rem(j, SLOTS)], hs_sems.at[SLOTS + lax.rem(j, RING)], sibling)

    def free(make, j, slots=SLOTS):
        @pl.when(j >= slots)
        def _():
            make(j - slots).wait_send()

    def mine(j, off, cols=slice(None)):
        q = chip_at(off)
        slot = lax.rem(j, p_own.shape[0])
        return p_own[slot, q, :, cols].astype(F32) + s_in[j, q, :, cols].astype(F32)

    def first(j):
        slot = lax.rem(j, 2)
        k, _ = where(j)

        @pl.when(j + 1 < items)
        def _():
            for c in up_load(j + 1):
                c.start()

        for i in range(1, nz):
            @pl.when(j == begins(i))
            def _():
                x_wait(i)
        for c in up_load(j):
            c.wait()
        free(sib, j, 2)
        for i in range(4):
            side = pl.ds(pl.multiple_of((core if i >= 2 else 1 - core) * hw, hw), hw)
            res = jnp.dot(xg[k], wgu[slot, i % 2, :, side], preferred_element_type=F32).astype(BF).reshape(n, g, hw)
            if i < 2:
                p_send[slot, :, :, pair_of[i]] = res
            else:
                p_own[lax.rem(j, p_own.shape[0]), :, :, pair_of[i - 2]] = res
            if i == 1:
                sib(j).start()

    def reduce_step(s, j):
        slot = lax.rem(j, SLOTS)
        if s == 0:
            sib(j).wait_recv()
        for d in range(2):
            free(functools.partial(rs, s, d), j)
            off = sign[d] * (hn - s)
            if s == 0:
                half_send[slot, d] = mine(j, off, pair_of[d]).astype(BF)
            else:
                rs(s - 1, d, j).wait_recv()
                if s == 1:
                    full_send[slot, 0, d, :, pair_of[1 - d]] = mine(j, off, pair_of[1 - d]).astype(BF)
                    full_send[slot, 0, d, :, pair_of[d]] = (
                        mine(j, off, pair_of[d]) + half_in[j, d].astype(F32)).astype(BF)
                else:
                    full_send[slot, s - 1, d] = (mine(j, off) + full_in[j, s - 2, d].astype(F32)).astype(BF)
            rs(s, d, j).start()

    def spread(k):
        at = lax.broadcasted_iota(jnp.int32, (g, mp), 1) - lax.broadcasted_iota(jnp.int32, (g, mp), 0)
        col = jnp.sum(jnp.where(at == me * g, scr[k], 0.0), axis=1, keepdims=True)
        scale[k] = jnp.broadcast_to(col, (g, 128))

    def glu(val):
        gate, up = val[:, :hw], val[:, hw:]
        return (gate / (1.0 + jnp.exp(-gate)) * up).astype(BF)

    def activate(j):
        k, _ = where(j)

        @pl.when(j == 0)
        def _():
            tot = ss[...]
            for d in range(1, nr):
                ss_copy(d).wait_recv()
                tot = tot + ssr[d - 1]
            scr[0] = lax.rsqrt(tot / (feat * nr) + 1e-5)
            for i in range(1, nz):
                scale_copy(i).start()
            spread(0)

        for i in range(1, nz):
            @pl.when(j == begins(i))
            def _():
                ref = scr.at[i]
                remote(ref, ref, sc_sems.at[0, i - 1], sc_sems.at[1, i - 1], {"col": plane(1)}).wait_recv()
                spread(i)
        for d in range(2):
            rs(hn - 1, d, j).wait_recv()
        val = mine(j, 0) + full_in[j, hn - 2, 0].astype(F32) + full_in[j, hn - 2, 1].astype(F32)
        h_all[j, core, me] = glu(val * scale[k][:, 0:1])
        for d in range(2):
            free(functools.partial(ag, 0, d), j)
            ag(0, d, j).start()

    def gather_step(s, j):
        for d in range(2):
            ag(s - 1, d, j, True).wait_recv()
            free(functools.partial(ag, s, d), j)
            ag(s, d, j).start()

    def gather_last(j):
        for d in range(2):
            ag(hn - 1, d, j, True).wait_recv()
        free(hs, j)
        hs(j).start()

    def project(j, k, wt):
        tile = 256
        for t in range(feat // tile):
            cols = slice(t * tile, (t + 1) * tile)
            res = jnp.dot(h_all[j, 0].reshape(m, hw), wt[:hw, cols], preferred_element_type=F32)
            res = res + jnp.dot(h_all[j, 1].reshape(m, hw), wt[hw:, cols], preferred_element_type=F32)
            acc[k, :, cols] += res

    def down(j):
        slot = lax.rem(j, 2)
        k, _ = where(j)

        @pl.when(j + 1 < late)
        def _():
            down_load(j + 1).start()
        down_load(j).wait()
        hs(j, True).wait_recv()
        project(j, k, wdn.at[slot])

    stages = [functools.partial(reduce_step, s) for s in range(hn)] + [activate]
    stages += [functools.partial(gather_step, s) for s in range(1, hn)] + [gather_last]
    near = [(1 + LAG * i, f) for i, f in enumerate(stages)]
    last = near[-1][0] + 1
    order = [(0, items, 0, first), (last, late, 0, down)]
    order = [(lag, late, 0, f) for lag, f in near[::-1]] + order

    def all_rs_copy(j, off):
        i = j - late
        return remote(all_send.at[i, off - 1], all_in.at[i, off - 1], all_rs.at[0, i, off - 1], all_rs.at[1, i, off - 1],
                      {"row": chip_at(off) * 2 + core})

    def all_ag_copy(j, off, flip, got=False):
        i = j - late
        at = 2 * off + flip - 1
        src = core + flip * (1 - 2 * core)
        ref = h_all.at[j, src if got else core, chip_at(-off) if got else me]
        return remote(ref, ref, all_ag.at[0, i, at], all_ag.at[1, i, at], {"row": chip_at(off) * 2 + src})

    far_first = sorted(range(1, n), key=lambda off: -min(off, n - off))
    everyone = [(off, flip) for off in far_first for flip in range(2)] + [(0, 1)]

    def late_load(j):
        i = j - late
        return pltpu.make_async_copy(
            wd_ref.at[pl.ds(pl.multiple_of(where(j)[1] * w, w), w)], wlast.at[i], wl_sem.at[i])

    def late_reduce(j):
        late_load(j).start()
        sib(j).wait_recv()
        for off in far_first:
            all_send[j - late, off - 1] = mine(j, off).astype(BF)
            all_rs_copy(j, off).start()

    def late_activate(j):
        k, _ = where(j)
        val = mine(j, 0)
        for off in range(1, n):
            all_rs_copy(j, off).wait_recv()
            val = val + all_in[j - late, off - 1].astype(F32)
        h_all[j, core, me] = glu(val * scale[k][:, 0:1])
        for off, flip in everyone:
            all_ag_copy(j, off, flip).start()

    def late_down(j):
        late_load(j).wait()
        for off, flip in everyone:
            all_ag_copy(j, off, flip, True).wait_recv()
        project(j, where(j)[0], wlast.at[j - late])

    tail = [(1, late_reduce), (1 + LAG, late_activate), (1 + 2 * LAG, late_down)]
    order += [(lag, items, late, f) for lag, f in tail[::-1]]
    steps = max(last + late, tail[-1][0] + items)

    def c_copy(k):
        return remote(cs.at[k - 1], cr.at[k - 1], c_sems.at[0, k - 1], c_sems.at[1, k - 1],
                      {"col": plane(k)})

    @pl.loop(0, steps)
    def _(t):
        for k in range(2, nz):
            @pl.when(t == begins(k - 1) )
            def _():
                x_copy(k).start()
        @pl.when(t == steps - 2)
        def _():
            for d in range(1, nr):
                ss_copy(d).wait_send()
            for k in range(1, nz):
                scale_copy(k).wait_send()
            for k in range(2, nz):
                c_copy(k).wait_recv()
                acc[0] += cr[k - 1].astype(F32)
        for lag, stop, start, stage in order:
            @pl.when((t >= start + lag) & (t - lag < stop))
            def _():
                stage(t - lag)

        @pl.when(t == 0)
        def _():
            squares()
        for k in range(1, nz):
            @pl.when(t == begins(k))
            def _():
                acc[k] = jnp.zeros_like(acc[k])

            @pl.when(t == ends(k) + last)
            def _():
                cs[k - 1] = acc[k].astype(BF)
                c_copy(k).start()

    res = acc[0]
    if nz > 1:
        c_copy(1).wait_recv()
        res = res + cr[0].astype(F32)
    out = res.astype(BF)
    out_ref[...] = out
    io_out.start()
    io_t.wait()
    diff = out.astype(F32) - teacher_ref[map_ref[0]].astype(F32)
    sq = jnp.sum((diff * diff).reshape(m // 8, 8, feat), axis=0)
    part = sq[:, 0:128]
    for c in range(1, feat // 128):
        part = part + sq[:, c * 128:(c + 1) * 128]

    def l_copy(axis, d):
        size, at = (nr, r) if axis == "row" else (nz, z)
        src, dst = (lsum.at[0], l_row) if axis == "row" else (lsum.at[1], l_col)
        sems = ss_sems if axis == "row" else sc_sems
        return remote(src, dst.at[d - 1], sems.at[0, d - 1], sems.at[1, d - 1],
                      {axis: lax.rem(at + d, size)})

    lsum[0] = part
    for d in range(1, nr):
        l_copy("row", d).start()
    for d in range(1, nr):
        l_copy("row", d).wait_recv()
        part = part + l_row[d - 1]
    lsum[1] = part
    for d in range(1, nz):
        l_copy("col", d).start()
    for d in range(1, nz):
        l_copy("col", d).wait_recv()
        part = part + l_col[d - 1]
    loss_ref[0, 0] = jnp.sum(part) / count

    for d in range(1, nr):
        l_copy("row", d).wait_send()
    for k in range(1, nz):
        l_copy("col", k).wait_send()
        x_copy(k).wait_send()
        c_copy(k).wait_send()
    for i in range(2):
        sib(jnp.int32(items - 2 + i)).wait_send()
    for i in range(items - late):
        j = jnp.int32(late + i)
        for off in range(1, n):
            all_rs_copy(j, off).wait_send()
        for off, flip in everyone:
            all_ag_copy(j, off, flip).wait_send()
    for i in range(SLOTS):
        j = jnp.int32(late - SLOTS + i)
        for d in range(2):
            for s in range(hn):
                rs(s, d, j).wait_send()
                ag(s, d, j).wait_send()
        hs(j).wait_send()
    io_out.wait()


def body(nr, nz, student_in, norm_gain, w_gate, w_up, w_down, teacher, layer_map):
    m, feat = student_in.shape
    ff = w_gate.shape[1]
    n, hn = nr // 2, nr // 4
    g = m // n
    mp = -(-m // 128) * 128
    w = next(v for v in (512, 256) if ff % v == 0)
    hw = w // 2
    chunks = ff // w
    c = nz * chunks
    lead = chunks // 2
    head = chunks - chunks // 3 - 1
    own = 1 + hn * LAG
    vm, dma = pltpu.VMEM, pltpu.SemaphoreType.DMA
    spec = pl.BlockSpec(memory_space=pltpu.VMEM)
    smem = pl.BlockSpec(memory_space=pltpu.SMEM)
    hbm = pl.BlockSpec(memory_space=pl.ANY)
    out, loss = pl.pallas_call(
        functools.partial(kernel, nr, nz, w, m * nz * feat * nr, lead, head),
        out_shape=(jax.ShapeDtypeStruct((m, feat), BF), jax.ShapeDtypeStruct((1, 1), F32)),
        in_specs=[hbm, spec, hbm, hbm, hbm, hbm, smem],
        out_specs=(hbm, smem),
        scratch_shapes=[
            vm((m, feat), BF),
            vm(teacher.shape, BF),
            vm((m, feat), BF),
            vm((nz, m, feat), BF),
            vm((1, mp), F32),
            vm((nr - 1, 1, mp), F32),
            vm((nz, 1, mp), F32),
            vm((nz, g, 128), F32),
            vm((2, 2, feat, w), BF),
            vm((2, w, feat), BF),
            vm((own, n, g, w), BF),
            vm((2, n, g, w), BF),
            vm((c, n, g, w), BF),
            vm((SLOTS, 2, g, hw), BF),
            vm((c, 2, g, hw), BF),
            vm((SLOTS, hn - 1, 2, g, w), BF),
            vm((c, hn - 1, 2, g, w), BF),
            vm((LATE, n - 1, g, w), BF),
            vm((LATE, n - 1, g, w), BF),
            vm((LATE, w, feat), BF),
            vm((c, 2, n, g, hw), BF),
            vm((nz, m, feat), F32),
            vm((nz - 1, m, feat), BF),
            vm((nz - 1, m, feat), BF),
            vm((2, 8, 128), F32),
            vm((nr - 1, 8, 128), F32),
            vm((nz - 1, 8, 128), F32),
            dma((2, nz - 1)),
            dma((2, 2)),
            dma((2,)),
            dma((2, nr - 1)),
            dma((2, nz - 1)),
            dma((2 + RING,)),
            dma((hn, 2, SLOTS)),
            dma((hn, 2, RING)),
            dma((hn, 2, SLOTS)),
            dma((hn, 2, RING)),
            dma((SLOTS + RING,)),
            dma((2, LATE, n - 1)),
            dma((2, LATE, nr - 1)),
            dma((LATE,)),
            dma((3,)),
            dma((2, nz - 1)),
        ],
        compiler_params=pltpu.CompilerParams(
            collective_id=0, has_side_effects=True, vmem_limit_bytes=67043328),
    )(student_in, norm_gain, w_gate, w_up, w_down, teacher, layer_map)
    return out, loss.reshape(())


def solution(mesh):
    placed = (
        P("col", "row"),
        P("row"),
        P("row", "col"),
        P("row", "col"),
        P("col", "row"),
        P(None, "col", "row"),
        P(),
    )
    return jax.shard_map(
        functools.partial(body, mesh.shape["row"], mesh.shape["col"]),
        mesh=mesh, in_specs=placed, out_specs=(P("col", "row"), P()), check_vma=False
    )
```

```python
import functools

import jax
import jax.numpy as jnp
from jax import lax
from jax.experimental import pallas as pl
from jax.experimental.pallas import tpu as pltpu
from jax.sharding import PartitionSpec as P

BF = jnp.bfloat16
F32 = jnp.float32
LAG = 2
SLOTS = 4
RING = 3 * LAG
LATE = 1


def kernel(nr, nz, w, count, lead, head, x_hbm, gain_ref, wg_ref, wu_ref, wd_ref, t_hbm, map_ref,
           out_hbm, loss_ref,
           x_ref, teacher_ref, out_ref, xg, ss, ssr, scr, scale, wgu, wdn, p_own, p_send, s_in, half_send, half_in,
           full_send, full_in, all_send, all_in, wlast, h_all, acc, cs, cr, lsum, l_row, l_col,
           x_sems, w_sem, wd_sem, ss_sems, sc_sems, sib_sems, rs_send, rs_recv, ag_send, ag_recv,
           hs_sems, all_rs, all_ag, wl_sem, io_sems, c_sems):
    items = s_in.shape[0]
    n = nr // 2
    hn = n // 2
    m, feat = x_ref.shape
    io_x = pltpu.make_async_copy(x_hbm, x_ref, io_sems.at[0])
    io_t = pltpu.make_async_copy(t_hbm, teacher_ref, io_sems.at[1])
    io_out = pltpu.make_async_copy(out_ref, out_hbm, io_sems.at[2])
    io_x.start()
    mp = ss.shape[-1]
    g = m // n
    hw = w // 2
    chunks = items // nz
    r = lax.axis_index("row")
    z = lax.axis_index("col")
    core = lax.rem(r, 2)
    chip = lax.div(r, 2)
    a, b = lax.div(chip, 2), lax.rem(chip, 2)
    pos = a + b * (n - 1 - 2 * a)

    def chip_at(off):
        q = lax.rem(pos + (off % n), n)
        far = lax.div(q, hn)
        return far * (2 * (n - 1 - q) + 1) + (1 - far) * 2 * q

    me = chip_at(0)
    sibling = {"row": chip * 2 + 1 - core}
    ring = ({"row": chip_at(1) * 2 + core}, {"row": chip_at(-1) * 2 + core})
    sign = (1, -1)
    pair_of = (slice(0, hw), slice(hw, w))
    unit_of = (pl.ds(0, hw // 2), pl.ds(hw // 2, hw // 2))
    late = items - all_in.shape[0]
    inner = (nz - 1) * chunks

    def plane(k, back=False):
        if nz & (nz - 1):
            return lax.rem(z + (nz - k if back else k), nz)
        q, bit = z, 1
        while bit <= k:
            if k & bit:
                q = q + bit * (1 - 2 * lax.rem(lax.div(z, bit), 2))
            bit *= 2
        return q

    def remote(src, dst, send, recv, dev):
        return pltpu.make_async_remote_copy(
            src_ref=src, dst_ref=dst, send_sem=send, recv_sem=recv,
            device_id=dev, device_id_type=pl.DeviceIdType.MESH)

    def where(j):
        part = lax.div(j + (inner - lead), inner)
        mid = lax.rem(part, 2)
        v = j - lead + (chunks - head)
        u = j + (chunks - lead) - lax.div(part, 2) * inner
        return (mid * (1 + lax.rem(lax.div(v, chunks), nz - 1)),
                mid * lax.rem(v, chunks) + (1 - mid) * lax.rem(u, chunks))

    def begins(k):
        return lead + (0 if k == 1 else head + (k - 2) * chunks)

    def ends(k):
        return lead + (inner if k == 1 else head + (k - 1) * chunks) - 1

    def up_load(j):
        slot = lax.rem(j, 2)
        copies = []
        cols = pl.ds(pl.multiple_of(where(j)[1] * w, w), w)
        for u, ref in enumerate((wg_ref, wu_ref)):
            copies.append(pltpu.make_async_copy(ref.at[:, cols], wgu.at[slot, u], w_sem.at[slot, u]))
        return copies

    def down_load(j):
        slot = lax.rem(j, 2)
        return pltpu.make_async_copy(
            wd_ref.at[pl.ds(pl.multiple_of(where(j)[1] * w, w), w)], wdn.at[slot], wd_sem.at[slot])

    for c in up_load(jnp.int32(0)):
        c.start()
    down_load(jnp.int32(0)).start()
    io_t.start()

    barrier = pltpu.get_barrier_semaphore()
    for d in range(1, nr):
        pl.semaphore_signal(barrier, inc=1, device_id={"row": lax.rem(r + d, nr)},
                            device_id_type=pl.DeviceIdType.MESH)
    for d in range(1, nz):
        pl.semaphore_signal(barrier, inc=1, device_id={"col": lax.rem(z + d, nz)},
                            device_id_type=pl.DeviceIdType.MESH)

    io_x.wait()

    xf = x_ref[...].astype(F32)
    xg[0] = (xf * gain_ref[...].astype(F32)[None, :]).astype(BF)
    pl.semaphore_wait(barrier, nr - 1 + nz - 1)

    def x_copy(k, back=False):
        return remote(xg.at[0], xg.at[k], x_sems.at[0, k - 1], x_sems.at[1, k - 1],
                      {"col": plane(k, not back)})

    def x_wait(k):
        ref = xg.at[k]
        remote(ref, ref, x_sems.at[0, k - 1], x_sems.at[1, k - 1], {"col": plane(1)}).wait_recv()

    def ss_copy(d):
        return remote(ss, ssr.at[d - 1], ss_sems.at[0, d - 1], ss_sems.at[1, d - 1],
                      {"row": lax.rem(r + d, nr)})

    def scale_copy(k):
        return remote(scr.at[0], scr.at[k], sc_sems.at[0, k - 1], sc_sems.at[1, k - 1],
                      {"col": plane(k, True)})

    if nz > 1:
        x_copy(1).start()

    def squares():
        xf = x_ref[...].astype(F32)
        sq = xf * xf
        part = sq[:, 0:128]
        for c in range(1, feat // 128):
            part = part + sq[:, c * 128:(c + 1) * 128]
        part = jnp.sum(part, axis=1, keepdims=True)
        same = lax.broadcasted_iota(jnp.int32, (m, mp), 0) == lax.broadcasted_iota(jnp.int32, (m, mp), 1)
        ss[...] = jnp.sum(jnp.where(same, part, 0.0), axis=0, keepdims=True)
        for d in range(1, nr):
            ss_copy(d).start()
        acc[0] = xf

    def sib(j):
        slot = lax.rem(j, 2)
        return remote(p_send.at[slot], s_in.at[j], sib_sems.at[slot], sib_sems.at[2 + lax.rem(j, RING)], sibling)

    def rs(s, d, j):
        slot = lax.rem(j, SLOTS)
        if s == 0:
            src, dst = half_send.at[slot, d], half_in.at[j, d]
        else:
            src, dst = full_send.at[slot, s - 1, d], full_in.at[j, s - 1, d]
        return remote(src, dst, rs_send.at[s, d, slot], rs_recv.at[s, d, lax.rem(j, RING)], ring[d])

    def ag(s, d, j, got=False):
        blk = chip_at(-sign[d] * (s + 1 if got else s))
        ref = h_all.at[j, core, blk]
        if s == hn - 1:
            ref = h_all.at[j, core, blk, :, unit_of[d]]
        return remote(ref, ref, ag_send.at[s, d, lax.rem(j, SLOTS)], ag_recv.at[s, d, lax.rem(j, RING)], ring[d])

    def hs(j, got=False):
        ref = h_all.at[j, 1 - core if got else core]
        return remote(ref, ref, hs_sems.at[lax.rem(j, SLOTS)], hs_sems.at[SLOTS + lax.rem(j, RING)], sibling)

    def free(make, j, slots=SLOTS):
        @pl.when(j >= slots)
        def _():
            make(j - slots).wait_send()

    def mine(j, off, cols=slice(None)):
        q = chip_at(off)
        slot = lax.rem(j, p_own.shape[0])
        return p_own[slot, q, :, cols].astype(F32) + s_in[j, q, :, cols].astype(F32)

    def first(j):
        slot = lax.rem(j, 2)
        k, _ = where(j)

        @pl.when(j + 1 < items)
        def _():
            for c in up_load(j + 1):
                c.start()

        for i in range(1, nz):
            @pl.when(j == begins(i))
            def _():
                x_wait(i)
        for c in up_load(j):
            c.wait()
        free(sib, j, 2)
        for i in range(4):
            side = pl.ds(pl.multiple_of((core if i >= 2 else 1 - core) * hw, hw), hw)
            res = jnp.dot(xg[k], wgu[slot, i % 2, :, side], preferred_element_type=F32).astype(BF).reshape(n, g, hw)
            if i < 2:
                p_send[slot, :, :, pair_of[i]] = res
            else:
                p_own[lax.rem(j, p_own.shape[0]), :, :, pair_of[i - 2]] = res
            if i == 1:
                sib(j).start()

    def reduce_step(s, j):
        slot = lax.rem(j, SLOTS)
        if s == 0:
            sib(j).wait_recv()
        for d in range(2):
            free(functools.partial(rs, s, d), j)
            off = sign[d] * (hn - s)
            if s == 0:
                half_send[slot, d] = mine(j, off, pair_of[d]).astype(BF)
            else:
                rs(s - 1, d, j).wait_recv()
                if s == 1:
                    full_send[slot, 0, d, :, pair_of[1 - d]] = mine(j, off, pair_of[1 - d]).astype(BF)
                    full_send[slot, 0, d, :, pair_of[d]] = (
                        mine(j, off, pair_of[d]) + half_in[j, d].astype(F32)).astype(BF)
                else:
                    full_send[slot, s - 1, d] = (mine(j, off) + full_in[j, s - 2, d].astype(F32)).astype(BF)
            rs(s, d, j).start()

    def spread(k):
        at = lax.broadcasted_iota(jnp.int32, (g, mp), 1) - lax.broadcasted_iota(jnp.int32, (g, mp), 0)
        col = jnp.sum(jnp.where(at == me * g, scr[k], 0.0), axis=1, keepdims=True)
        scale[k] = jnp.broadcast_to(col, (g, 128))

    def glu(val):
        gate, up = val[:, :hw], val[:, hw:]
        return (gate / (1.0 + jnp.exp(-gate)) * up).astype(BF)

    def activate(j):
        k, _ = where(j)

        @pl.when(j == 0)
        def _():
            tot = ss[...]
            for d in range(1, nr):
                ss_copy(d).wait_recv()
                tot = tot + ssr[d - 1]
            scr[0] = lax.rsqrt(tot / (feat * nr) + 1e-5)
            for i in range(1, nz):
                scale_copy(i).start()
            spread(0)

        for i in range(1, nz):
            @pl.when(j == begins(i))
            def _():
                ref = scr.at[i]
                remote(ref, ref, sc_sems.at[0, i - 1], sc_sems.at[1, i - 1], {"col": plane(1)}).wait_recv()
                spread(i)
        for d in range(2):
            rs(hn - 1, d, j).wait_recv()
        val = mine(j, 0) + full_in[j, hn - 2, 0].astype(F32) + full_in[j, hn - 2, 1].astype(F32)
        h_all[j, core, me] = glu(val * scale[k][:, 0:1])
        for d in range(2):
            free(functools.partial(ag, 0, d), j)
            ag(0, d, j).start()

    def gather_step(s, j):
        for d in range(2):
            ag(s - 1, d, j, True).wait_recv()
            free(functools.partial(ag, s, d), j)
            ag(s, d, j).start()

    def gather_last(j):
        for d in range(2):
            ag(hn - 1, d, j, True).wait_recv()
        free(hs, j)
        hs(j).start()

    def project(j, k, wt):
        tile = 256
        for t in range(feat // tile):
            cols = slice(t * tile, (t + 1) * tile)
            res = jnp.dot(h_all[j, 0].reshape(m, hw), wt[:hw, cols], preferred_element_type=F32)
            res = res + jnp.dot(h_all[j, 1].reshape(m, hw), wt[hw:, cols], preferred_element_type=F32)
            acc[k, :, cols] += res

    def down(j):
        slot = lax.rem(j, 2)
        k, _ = where(j)

        @pl.when(j + 1 < late)
        def _():
            down_load(j + 1).start()
        down_load(j).wait()
        hs(j, True).wait_recv()
        project(j, k, wdn.at[slot])

    stages = [functools.partial(reduce_step, s) for s in range(hn)] + [activate]
    stages += [functools.partial(gather_step, s) for s in range(1, hn)] + [gather_last]
    near = [(1 + LAG * i, f) for i, f in enumerate(stages)]
    last = near[-1][0] + 1
    order = [(0, items, 0, first), (last, late, 0, down)]
    order = [(lag, late, 0, f) for lag, f in near[::-1]] + order

    def all_rs_copy(j, off):
        i = j - late
        return remote(all_send.at[i, off - 1], all_in.at[i, off - 1], all_rs.at[0, i, off - 1], all_rs.at[1, i, off - 1],
                      {"row": chip_at(off) * 2 + core})

    def all_ag_copy(j, off, flip, got=False):
        i = j - late
        at = 2 * off + flip - 1
        src = core + flip * (1 - 2 * core)
        ref = h_all.at[j, src if got else core, chip_at(-off) if got else me]
        return remote(ref, ref, all_ag.at[0, i, at], all_ag.at[1, i, at], {"row": chip_at(off) * 2 + src})

    far_first = sorted(range(1, n), key=lambda off: -min(off, n - off))
    everyone = [(off, flip) for off in far_first for flip in range(2)] + [(0, 1)]

    def late_load(j):
        i = j - late
        return pltpu.make_async_copy(
            wd_ref.at[pl.ds(pl.multiple_of(where(j)[1] * w, w), w)], wlast.at[i], wl_sem.at[i])

    def late_reduce(j):
        late_load(j).start()
        sib(j).wait_recv()
        for off in far_first:
            all_send[j - late, off - 1] = mine(j, off).astype(BF)
            all_rs_copy(j, off).start()

    def late_activate(j):
        k, _ = where(j)
        val = mine(j, 0)
        for off in range(1, n):
            all_rs_copy(j, off).wait_recv()
            val = val + all_in[j - late, off - 1].astype(F32)
        h_all[j, core, me] = glu(val * scale[k][:, 0:1])
        for off, flip in everyone:
            all_ag_copy(j, off, flip).start()

    def late_down(j):
        late_load(j).wait()
        for off, flip in everyone:
            all_ag_copy(j, off, flip, True).wait_recv()
        project(j, where(j)[0], wlast.at[j - late])

    tail = [(1, late_reduce), (1 + LAG, late_activate), (1 + 2 * LAG, late_down)]
    order += [(lag, items, late, f) for lag, f in tail[::-1]]
    steps = max(last + late, tail[-1][0] + items)

    def c_copy(k):
        return remote(cs.at[k - 1], cr.at[k - 1], c_sems.at[0, k - 1], c_sems.at[1, k - 1],
                      {"col": plane(k)})

    def add_block(k):
        if k < nz:
            c_copy(k).wait_recv()
            acc[0] += cr[k - 1].astype(F32)

    @pl.loop(0, steps)
    def _(t):
        for k in range(2, nz):
            @pl.when(t == begins(k - 1) )
            def _():
                x_copy(k).start()
        @pl.when(t == steps - 2)
        def _():
            for d in range(1, nr):
                ss_copy(d).wait_send()
            for k in range(1, nz):
                scale_copy(k).wait_send()
            add_block(max(2, nz - 1))

        @pl.when(t == items)
        def _():
            for k in range(2, nz - 1):
                add_block(k)
        for lag, stop, start, stage in order:
            @pl.when((t >= start + lag) & (t - lag < stop))
            def _():
                stage(t - lag)

        @pl.when(t == 1)
        def _():
            squares()
        for k in range(1, nz):
            @pl.when(t == begins(k))
            def _():
                acc[k] = jnp.zeros_like(acc[k])

            @pl.when(t == ends(k) + last)
            def _():
                cs[k - 1] = acc[k].astype(BF)
                c_copy(k).start()

    res = acc[0]
    if nz > 1:
        c_copy(1).wait_recv()
        res = res + cr[0].astype(F32)
    out = res.astype(BF)
    out_ref[...] = out
    io_out.start()
    io_t.wait()
    diff = out.astype(F32) - teacher_ref[map_ref[0]].astype(F32)
    sq = jnp.sum((diff * diff).reshape(m // 8, 8, feat), axis=0)
    part = sq[:, 0:128]
    for c in range(1, feat // 128):
        part = part + sq[:, c * 128:(c + 1) * 128]

    def l_copy(axis, d):
        size, at = (nr, r) if axis == "row" else (nz, z)
        src, dst = (lsum.at[0], l_row) if axis == "row" else (lsum.at[1], l_col)
        sems = ss_sems if axis == "row" else sc_sems
        return remote(src, dst.at[d - 1], sems.at[0, d - 1], sems.at[1, d - 1],
                      {axis: lax.rem(at + d, size)})

    lsum[0] = part
    for d in range(1, nr):
        l_copy("row", d).start()
    for k in range(1, nz):
        x_copy(k).wait_send()
        c_copy(k).wait_send()
    for i in range(2):
        sib(jnp.int32(items - 2 + i)).wait_send()
    for i in range(items - late):
        j = jnp.int32(late + i)
        for off in range(1, n):
            all_rs_copy(j, off).wait_send()
        for off, flip in everyone:
            all_ag_copy(j, off, flip).wait_send()
    for i in range(SLOTS):
        j = jnp.int32(late - SLOTS + i)
        for d in range(2):
            for s in range(hn):
                rs(s, d, j).wait_send()
                ag(s, d, j).wait_send()
        hs(j).wait_send()
    for d in range(1, nr):
        l_copy("row", d).wait_recv()
        part = part + l_row[d - 1]
    lsum[1] = part
    for d in range(1, nz):
        l_copy("col", d).start()
    for d in range(1, nz):
        l_copy("col", d).wait_recv()
        part = part + l_col[d - 1]
    loss_ref[0, 0] = jnp.sum(part) / count

    for d in range(1, nr):
        l_copy("row", d).wait_send()
    for k in range(1, nz):
        l_copy("col", k).wait_send()
    io_out.wait()


def body(nr, nz, student_in, norm_gain, w_gate, w_up, w_down, teacher, layer_map):
    m, feat = student_in.shape
    ff = w_gate.shape[1]
    n, hn = nr // 2, nr // 4
    g = m // n
    mp = -(-m // 128) * 128
    w = next(v for v in (512, 256) if ff % v == 0)
    hw = w // 2
    chunks = ff // w
    c = nz * chunks
    lead = chunks // 2
    head = chunks - chunks // 3 - 1
    own = 1 + hn * LAG
    vm, dma = pltpu.VMEM, pltpu.SemaphoreType.DMA
    spec = pl.BlockSpec(memory_space=pltpu.VMEM)
    smem = pl.BlockSpec(memory_space=pltpu.SMEM)
    hbm = pl.BlockSpec(memory_space=pl.ANY)
    out, loss = pl.pallas_call(
        functools.partial(kernel, nr, nz, w, m * nz * feat * nr, lead, head),
        out_shape=(jax.ShapeDtypeStruct((m, feat), BF), jax.ShapeDtypeStruct((1, 1), F32)),
        in_specs=[hbm, spec, hbm, hbm, hbm, hbm, smem],
        out_specs=(hbm, smem),
        scratch_shapes=[
            vm((m, feat), BF),
            vm(teacher.shape, BF),
            vm((m, feat), BF),
            vm((nz, m, feat), BF),
            vm((1, mp), F32),
            vm((nr - 1, 1, mp), F32),
            vm((nz, 1, mp), F32),
            vm((nz, g, 128), F32),
            vm((2, 2, feat, w), BF),
            vm((2, w, feat), BF),
            vm((own, n, g, w), BF),
            vm((2, n, g, w), BF),
            vm((c, n, g, w), BF),
            vm((SLOTS, 2, g, hw), BF),
            vm((c, 2, g, hw), BF),
            vm((SLOTS, hn - 1, 2, g, w), BF),
            vm((c, hn - 1, 2, g, w), BF),
            vm((LATE, n - 1, g, w), BF),
            vm((LATE, n - 1, g, w), BF),
            vm((LATE, w, feat), BF),
            vm((c, 2, n, g, hw), BF),
            vm((nz, m, feat), F32),
            vm((nz - 1, m, feat), BF),
            vm((nz - 1, m, feat), BF),
            vm((2, 8, 128), F32),
            vm((nr - 1, 8, 128), F32),
            vm((nz - 1, 8, 128), F32),
            dma((2, nz - 1)),
            dma((2, 2)),
            dma((2,)),
            dma((2, nr - 1)),
            dma((2, nz - 1)),
            dma((2 + RING,)),
            dma((hn, 2, SLOTS)),
            dma((hn, 2, RING)),
            dma((hn, 2, SLOTS)),
            dma((hn, 2, RING)),
            dma((SLOTS + RING,)),
            dma((2, LATE, n - 1)),
            dma((2, LATE, nr - 1)),
            dma((LATE,)),
            dma((3,)),
            dma((2, nz - 1)),
        ],
        compiler_params=pltpu.CompilerParams(
            collective_id=0, has_side_effects=True, vmem_limit_bytes=67043328),
    )(student_in, norm_gain, w_gate, w_up, w_down, teacher, layer_map)
    return out, loss.reshape(())


def solution(mesh):
    placed = (
        P("col", "row"),
        P("row"),
        P("row", "col"),
        P("row", "col"),
        P("col", "row"),
        P(None, "col", "row"),
        P(),
    )
    return jax.shard_map(
        functools.partial(body, mesh.shape["row"], mesh.shape["col"]),
        mesh=mesh, in_specs=placed, out_specs=(P("col", "row"), P()), check_vma=False
    )
```
